256 devices in a mesh: rep: 32 (over x_hi, z, core), tp: 8 (over x_lo, y).
Axes of the slice: x: 4 (x_hi: 2, x_lo: 2; x = x_hi * 2 + x_lo), y: 4, z: 8, core: 2. Of those that a mesh axis runs over, the one named last changes fastest.
Arguments:
- hidden: bfloat16 [4, 2048, 8192], P(None, 'rep', 'tp'), may hold values from -6 to 6
- query_base: bfloat16 [4, 2048, 8192], P(None, 'rep', 'tp'), may hold values from -13 to 13
- kv_base: bfloat16 [4, 2048, 2, 1024], P(None, 'rep', None, 'tp'), may hold values from -6 to 6
- kv_cache: bfloat16 [2048, 128, 2, 1024], P('rep', None, None, 'tp'), may hold values from -13 to 13
- cache_lengths: int32 [2048], P('rep'), may hold values from 2 to 124
- adapter_ids: int32 [4, 2048], P(None, 'rep'), may hold values from 0 to 5, as said below
- migrating: int32 [4, 64], P(None, 'rep'), may hold values from 0 to 63, as said below
- pair_mask: int32 [4], replicated, may hold values from 1 to 16, as said below
- owners: int32 [4], replicated, may hold values from 0 to 31, as said below
- pool_down: bfloat16 [2, 2, 64, 8192], P(None, None, None, 'tp'), may hold values from -0.0625 to 0.0625
- pool_upq: bfloat16 [2, 64, 8192], P(None, None, 'tp'), may hold values from -0.75 to 0.75
- pool_upv: bfloat16 [2, 64, 1024], P(None, None, 'tp'), may hold values from -0.75 to 0.75
- store_down: bfloat16 [32, 2, 64, 8192], P('rep', None, None, 'tp'), may hold values from -0.0625 to 0.0625
- store_upq: bfloat16 [32, 64, 8192], P('rep', None, 'tp'), may hold values from -0.75 to 0.75
- store_upv: bfloat16 [32, 64, 1024], P('rep', None, 'tp'), may hold values from -0.75 to 0.75
Outputs:
- attention: bfloat16 [4, 2048, 8192], P(None, 'rep', 'tp')
The draws below stay inside these ranges and needn't reach their ends.
Inputs may be any that keep to these rules, and one draw needn't show every extreme that they name: The 4 owners are distinct replicas. `migrating`: at one step the 2 entries of one replica are distinct slots. `adapter_ids`: at step s every entry is at most 2 + s. `pair_mask`: every entry is a power of two.
All inputs are finite; a program needn't handle non-finite values.
Results may differ from the reference program's by a relative error of at most 0.0064.
Values may be sent and summed in bfloat16 or wider, within the bound.
No kernel may reach another device: no remote copies, remote signals or barrier semaphores. Data moves between devices by JAX's collectives and lax.ppermute only.
A program may use at most 128 MiB of HBM per device.

```python
import math
import jax
import jax.numpy as jnp
from jax import lax

D = 8192
HEADS = 64
KVH = 8
HD = 128
RANK = 64
POOL = 2
STEPS = 4
MIG = 2
CTX = 128
REQ = 64
ROWS = 2048
N_REP = 32


def draw_query_base(key, part):
    shape_all = (STEPS, ROWS, HEADS * HD)
    base = jnp.clip(jax.random.normal(jax.random.fold_in(key, 1), shape_all, jnp.float32), -6.0, 6.0)
    return base.astype(jnp.bfloat16)


def draw_kv_cache(key, part):
    shape_all = (ROWS, CTX, 2, KVH * HD)
    base = jnp.clip(jax.random.normal(jax.random.fold_in(key, 2), shape_all, jnp.float32), -6.0, 6.0)
    return base.astype(jnp.bfloat16)


def draw_owners(key, part):
    rest = jax.random.permutation(jax.random.fold_in(key, 21), N_REP - 1)[:STEPS - 1]
    full = jnp.concatenate([rest.astype(jnp.int32), jnp.array([N_REP - 1], dtype=jnp.int32)])
    order = jax.random.permutation(jax.random.fold_in(key, 22), STEPS)
    return full[order].astype(jnp.int32)


def draw_pair_mask(key, part):
    bit_count = N_REP.bit_length() - 1
    exponents = jax.random.randint(jax.random.fold_in(key, 51), (STEPS,), 0, bit_count).astype(jnp.int32)
    exponents = exponents.at[0].set(0).at[1].set(bit_count - 1)
    order = jax.random.permutation(jax.random.fold_in(key, 52), STEPS)
    exponents = exponents[order]
    return jnp.left_shift(jnp.ones((STEPS,), jnp.int32), exponents).astype(jnp.int32)


def first_slots(sub_key):
    return jax.random.permutation(sub_key, REQ)[:MIG]


def draw_migrating(key, part):
    sub_keys = jax.random.split(jax.random.fold_in(key, 31), STEPS * N_REP)
    slots = jax.vmap(first_slots)(sub_keys)
    return slots.reshape(STEPS, N_REP * MIG).astype(jnp.int32)


def draw_adapter_ids(key, part):
    ceiling = (POOL + 1 + jnp.arange(STEPS, dtype=jnp.int32))[:, None]
    return jax.random.randint(jax.random.fold_in(key, 41), (STEPS, ROWS), 0, ceiling).astype(jnp.int32)


def set_ends(entries, own_key, least, top_value):
    shape = entries.shape
    place = [jax.random.randint(jax.random.fold_in(own_key, axis), (), 0, shape[axis]) for axis in range(len(shape))]
    entries = entries.at[tuple(place)].set(least)
    longest = shape.index(max(shape))
    place[longest] = (place[longest] + 1) % shape[longest]
    return entries.at[tuple(place)].set(top_value)


def block_levels(stream_key, dims, cuts, low, largest):
    loudness = 1.0
    for axis_at, blocks in cuts:
        heights = jax.random.uniform(jax.random.fold_in(jax.random.fold_in(stream_key, 6), axis_at), (blocks,), jnp.float32, low / len(cuts), largest / len(cuts))
        loudness = loudness * jnp.repeat(jnp.exp(heights), dims[axis_at] // blocks).reshape((-1,) + (1,) * (len(dims) - 1 - axis_at))
    return loudness


def centred(stream_key, dims, scale, limit, cuts=(), kind=jnp.bfloat16):
    values = scale * jax.random.normal(stream_key, dims, jnp.float32)
    if cuts:
        values = values * block_levels(stream_key, dims, cuts, -0.22, 0.18)
    return jnp.clip(values, -limit, limit).astype(kind)


def setup_inputs(seed: int = 0) -> dict:
    key_list = jax.random.split(jax.random.key(seed), 16)
    return {
        "hidden": centred(key_list[0], (STEPS, ROWS, D), 1.0, 6.0, ((1, 32), (2, 8))),
        "query_base": draw_query_base(jax.random.fold_in(key_list[15], 71), 0),
        "kv_base": centred(key_list[2], (STEPS, ROWS, 2, KVH * HD), 1.0, 6.0, ((1, 32), (3, 8))),
        "kv_cache": draw_kv_cache(jax.random.fold_in(key_list[15], 71), 0),
        "cache_lengths": set_ends(jax.random.randint(key_list[4], (ROWS,), 2, CTX - STEPS + 1), jax.random.fold_in(key_list[4], 1), 2, CTX - STEPS).astype(jnp.int32),
        "adapter_ids": draw_adapter_ids(jax.random.fold_in(key_list[15], 71), 0),
        "migrating": draw_migrating(jax.random.fold_in(key_list[15], 71), 0),
        "pair_mask": draw_pair_mask(jax.random.fold_in(key_list[15], 71), 0),
        "owners": draw_owners(jax.random.fold_in(key_list[15], 71), 0),
        "pool_down": centred(key_list[9], (POOL, 2, RANK, D), D ** -0.5, 0.0625, ((3, 8),)),
        "pool_upq": centred(key_list[10], (POOL, RANK, HEADS * HD), RANK ** -0.5, 0.75, ((2, 8),)),
        "pool_upv": centred(key_list[11], (POOL, RANK, KVH * HD), RANK ** -0.5, 0.75, ((2, 8),)),
        "store_down": centred(key_list[12], (N_REP, 2, RANK, D), D ** -0.5, 0.0625, ((0, 32), (3, 8))),
        "store_upq": centred(key_list[13], (N_REP, RANK, HEADS * HD), RANK ** -0.5, 0.75, ((0, 32), (2, 8))),
        "store_upv": centred(key_list[14], (N_REP, RANK, KVH * HD), RANK ** -0.5, 0.75, ((0, 32), (2, 8))),
    }


def attend(query_rows, kv_rows, lengths, head_dim):
    req_count = kv_rows.shape[0]
    ctx_len = kv_rows.shape[1]
    kv_local = kv_rows.shape[3] // head_dim
    group_size = query_rows.shape[1] // (kv_local * head_dim)
    heads_q = query_rows.astype(jnp.float32).reshape(req_count, kv_local, group_size, head_dim)
    key_rows = kv_rows[:, :, 0].astype(jnp.float32).reshape(req_count, ctx_len, kv_local, head_dim)
    value_rows = kv_rows[:, :, 1].astype(jnp.float32).reshape(req_count, ctx_len, kv_local, head_dim)
    scores = jnp.einsum('rkgd,rckd->rkgc', heads_q, key_rows) / math.sqrt(head_dim)
    valid_mask = jnp.arange(ctx_len, dtype=jnp.int32)[None, :] <= lengths[:, None]
    scores = jnp.where(valid_mask[:, None, None, :], scores, -1e+30)
    row_peak = lax.optimization_barrier(jnp.max(scores, axis=-1, keepdims=True))
    exp_scores = jnp.exp(scores - row_peak)
    weights = (exp_scores / lax.optimization_barrier(jnp.sum(exp_scores, axis=-1, keepdims=True))).astype(jnp.bfloat16)
    mixed_out = jnp.einsum('rkgc,rckd->rkgd', weights.astype(jnp.float32), value_rows)
    return mixed_out.astype(jnp.bfloat16).reshape(req_count, -1)

def reference(hidden, query_base, kv_base, kv_cache, cache_lengths, adapter_ids, migrating, pair_mask, owners, pool_down, pool_upq, pool_upv, store_down, store_upq, store_upv):
    down_all = jnp.concatenate([pool_down, store_down[owners]], axis=0)
    upq_all = jnp.concatenate([pool_upq, store_upq[owners]], axis=0)
    upv_all = jnp.concatenate([pool_upv, store_upv[owners]], axis=0)
    slots_all = POOL + STEPS
    row_count = hidden.shape[1]
    replica_ids = jnp.arange(N_REP, dtype=jnp.int32)
    kv_state = kv_cache
    lengths = cache_lengths
    outputs = []

    def per_replica(block):
        return attend(block[0], block[1], block[2], HD)
    for step_num in range(STEPS):
        partner = jnp.bitwise_xor(replica_ids, pair_mask[step_num])
        slot_table = migrating[step_num].reshape(N_REP, MIG)
        target = (replica_ids[:, None] * REQ + slot_table).reshape(-1).astype(jnp.int32)
        source = (partner[:, None] * REQ + slot_table[partner]).reshape(-1).astype(jnp.int32)
        moved_rows = kv_state[source]
        moved_len = lengths[source]
        kv_state = kv_state.at[target].set(moved_rows)
        lengths = lengths.at[target].set(moved_len)
        tokens = hidden[step_num]
        partial_sum = jnp.dot(tokens, down_all.reshape(-1, D).T, preferred_element_type=jnp.float32)
        partial_sum = partial_sum.reshape(row_count, slots_all, 2, RANK)
        picker = (adapter_ids[step_num][:, None] == jnp.arange(slots_all, dtype=jnp.int32)[None, :]).astype(jnp.float32)
        low_rank = lax.optimization_barrier(jnp.sum(picker[:, :, None, None] * partial_sum, axis=1)).astype(jnp.bfloat16)
        spread = picker.astype(jnp.bfloat16)[:, :, None, None] * low_rank[:, None]
        delta_q = jnp.dot(spread[:, :, 0].reshape(row_count, -1), upq_all.reshape(-1, HEADS * HD), preferred_element_type=jnp.float32)
        delta_v = jnp.dot(spread[:, :, 1].reshape(row_count, -1), upv_all.reshape(-1, KVH * HD), preferred_element_type=jnp.float32)
        query_rows = (query_base[step_num].astype(jnp.float32) + delta_q).astype(jnp.bfloat16)
        new_value = (kv_base[step_num][:, 1].astype(jnp.float32) + delta_v).astype(jnp.bfloat16)
        fresh_rows = jnp.stack([kv_base[step_num][:, 0], new_value], axis=1)
        kv_state = kv_state.at[jnp.arange(row_count, dtype=jnp.int32), lengths].set(fresh_rows)
        blocks = (query_rows.reshape(N_REP, REQ, HEADS * HD), kv_state.reshape(N_REP, REQ, CTX, 2, KVH * HD), lengths.reshape(N_REP, REQ))
        result = lax.map(per_replica, blocks)
        outputs.append(result.reshape(row_count, HEADS * HD))
        lengths = lengths + 1
    return jnp.stack(outputs, axis=0)
```

```python
import math

import jax
import jax.numpy as jnp
from jax import lax
from jax.experimental import pallas as pl
from jax.experimental.pallas import tpu as pltpu
from jax.sharding import PartitionSpec as P

STEPS = 4
MIG = 2
POOL = 2
SLOTS = POOL + STEPS
REQ = 64
CTX = 128
HD = 128
HEADS = 8
D = 1024
RANK = 64
TOK = STEPS * REQ
GHOST = 16
ROWS = TOK + GHOST
MSG = 288
KV = 2 * CTX
PIECE = 56
F32 = jnp.float32
BF = jnp.bfloat16
NT = (((1,), (1,)), ((), ()))


VM = pl.BlockSpec(memory_space=pltpu.VMEM)
SM = pl.BlockSpec(memory_space=pltpu.SMEM)
ANY = pl.BlockSpec(memory_space=pl.ANY)

GHOSTS = [(s, j, t) for s in range(1, STEPS) for j in range(MIG) for t in range(s)]


def call(kernel, name, out_shape, in_specs, scratch=(), flops=0, nbytes=0):
    return pl.pallas_call(
        kernel,
        name=name,
        out_shape=out_shape,
        in_specs=in_specs,
        out_specs=VM,
        scratch_shapes=list(scratch),
        cost_estimate=pl.CostEstimate(flops=flops, bytes_accessed=nbytes, transcendentals=0),
    )


def pack_kernel(down, upq, upv, out):
    for k in range(2):
        for p in range(16):
            g, b = p // 4, p % 4
            j = (p // 8) * 16 + (p % 8) * 2 + k
            cols = slice(512 * k + 128 * b, 512 * k + 128 * b + 128)
            out[j, 0:32, :] = down[32 * g : 32 * g + 32, cols]
            out[j, 32:48, :] = upq[16 * g : 16 * g + 16, cols]
            out[j, 48:56, :] = upv[8 * (p % 8) : 8 * (p % 8) + 8, :]


def pick_kernel(owners, got, out):
    for s in range(STEPS):
        piece = got[owners[s]]
        for p in range(16):
            out[p, s] = piece


def message_kernel(slots, kv_hbm, hidden, kvb, meta, out, tail, sem):
    copies = [
        pltpu.make_async_copy(kv_hbm.at[slots[m]], out.at[m, pl.ds(0, KV)], sem.at[m])
        for m in range(STEPS * MIG)
    ]
    for copy in copies:
        copy.start()
    n = STEPS * MIG
    row = lax.broadcasted_iota(jnp.int32, (n, 128), 0)
    lane = lax.broadcasted_iota(jnp.int32, (n, 128), 1)
    slot = jnp.zeros((n, 128), jnp.int32)
    for m in range(n):
        slot = jnp.where(row == m, slots[m], slot)
    one = jnp.where(lane == slot, 1.0, 0.0).astype(BF)[:, :REQ]
    key = jnp.where(lane == 2 * slot, 1.0, 0.0).astype(BF)
    val = jnp.where(lane == 2 * slot + 1, 1.0, 0.0).astype(BF)
    for t in range(STEPS - 1):
        picked = jnp.dot(one, hidden[REQ * t : REQ * t + REQ, :], preferred_element_type=F32)
        for b in range(8):
            tail[pl.ds(8 * t + b, n, stride=32), :] = picked[:, 128 * b : 128 * b + 128]
        base = kvb[128 * t : 128 * t + 128, :]
        tail[pl.ds(24 + 2 * t, n, stride=32), :] = jnp.dot(key, base, preferred_element_type=F32)
        tail[pl.ds(25 + 2 * t, n, stride=32), :] = jnp.dot(val, base, preferred_element_type=F32)
    tail[pl.ds(30, n, stride=32), :] = jnp.dot(one, meta[...], preferred_element_type=F32)
    tail[pl.ds(31, n, stride=32), :] = jnp.zeros((n, 128), F32)
    for m in range(n):
        out[m, KV:MSG, :] = tail[32 * m : 32 * m + 32, :].astype(BF)
    for copy in copies:
        copy.wait()


def project_kernel(core, hidden, arr1, arr2, arr3, ids, pool, own, oth, out, w, x, gx):
    w[0 : POOL * 128, :] = pool[...]
    mine = core[0] * 512
    theirs = 512 - mine
    for s in range(STEPS):
        for p in range(16):
            g, b = p // 4, p % 4
            rows = slice((POOL + s) * 128 + 32 * g, (POOL + s) * 128 + 32 * g + 32)
            w[rows, pl.ds(pl.multiple_of(mine + 128 * b, 128), 128)] = own[p, s, 0:32, :]
            w[rows, pl.ds(pl.multiple_of(theirs + 128 * b, 128), 128)] = oth[p, s, 0:32, :]
    x[0:TOK, :] = hidden[...]
    gx[...] = jnp.zeros_like(gx)
    arrived = (None, arr1, arr2, arr3)
    for g, (s, j, t) in enumerate(GHOSTS):
        history = arrived[s][j, KV : KV + 32, :].astype(F32)
        for b in range(8):
            gx[g : g + 1, 128 * b : 128 * b + 128] = history[8 * t + b : 8 * t + b + 1, :]
    x[TOK:ROWS, :] = gx[...].astype(BF)
    total = jnp.zeros((ROWS, 128), F32)
    for a in range(SLOTS):
        part = lax.dot_general(x[...], w[128 * a : 128 * a + 128, :], NT, preferred_element_type=F32)
        total = jnp.where(ids[...] == a, part, total)
    total = total.astype(BF)
    for c in range(8):
        out[c] = total


def attend_kernel(
    scal, parts, ids, pool_q, pool_v, own, oth, qb, kvb, kv_hbm, arr0, arr1, arr2, arr3,
    out, kv, wq, wv, qs, os, ts, base, dv, tails, sem,
):
    copies = [
        pltpu.make_async_copy(kv_hbm.at[pl.ds(8 * b, 8)], kv.at[pl.ds(8 * b, 8)], sem.at[b])
        for b in range(8)
    ]
    for copy in copies:
        copy.start()
    arrived = (arr0, arr1, arr2, arr3)

    core = scal[REQ + 2 * STEPS * MIG]
    mine = core * 512
    theirs = 512 - mine
    for a in range(SLOTS):
        wq[128 * a + RANK : 128 * a + 128, :] = jnp.zeros((RANK, D), BF)
        wv[128 * a : 128 * a + RANK, :] = jnp.zeros((RANK, HD), BF)
    for a in range(POOL):
        wq[128 * a : 128 * a + RANK, :] = pool_q[RANK * a : RANK * a + RANK, :]
        wv[128 * a + RANK : 128 * a + 128, :] = pool_v[RANK * a : RANK * a + RANK, :]
    for s in range(STEPS):
        top = 128 * (POOL + s)
        for p in range(16):
            g, b = p // 4, p % 4
            rows = slice(top + 16 * g, top + 16 * g + 16)
            wq[rows, pl.ds(pl.multiple_of(mine + 128 * b, 128), 128)] = own[p, s, 32:48, :]
            wq[rows, pl.ds(pl.multiple_of(theirs + 128 * b, 128), 128)] = oth[p, s, 32:48, :]
        for p in range(8):
            wv[top + RANK + 8 * p : top + RANK + 8 * p + 8, :] = own[p, s, 48:56, :]

    u = parts[0].astype(F32)
    for c in range(1, 8):
        u = u + parts[c].astype(F32)
    spread = jnp.concatenate([jnp.where(ids[...] == a, u, 0.0).astype(BF) for a in range(SLOTS)], axis=1)
    dv[...] = jnp.dot(spread, wv[...], preferred_element_type=F32)
    dq = jnp.dot(spread[:TOK], wq[...], preferred_element_type=F32)
    base[...] = kvb[...].astype(F32)
    for t in range(STEPS):
        for h in range(HEADS):
            cols = slice(HD * h, HD * h + HD)
            query = qb[REQ * t : REQ * t + REQ, cols].astype(F32) + dq[REQ * t : REQ * t + REQ, cols]
            qs[pl.ds(8 * t + h, REQ, stride=32), :] = query
        ts[pl.ds(2 * t, REQ, stride=8), :] = base[pl.ds(128 * t, REQ, stride=2), :]
        ts[pl.ds(2 * t + 1, REQ, stride=8), :] = (
            base[pl.ds(128 * t + 1, REQ, stride=2), :] + dv[REQ * t : REQ * t + REQ, :]
        )

    col = lax.broadcasted_iota(jnp.int32, (32, KV), 1)
    step_of = lax.broadcasted_iota(jnp.int32, (32, KV), 0) // HEADS
    reach = jnp.where(col % 2 == 0, col - 2 * step_of, 4 * KV)
    row32 = lax.broadcasted_iota(jnp.int32, (32, HD), 0)
    row8 = lax.broadcasted_iota(jnp.int32, (8, HD), 0)

    def one(i, slot, length, tok):
        first = 2 * length
        start = pl.multiple_of(jnp.minimum((first // 16) * 16, KV - 32), 16)
        off = first - start
        turned = pltpu.roll(tok, off % 8, 0)
        turned = jnp.concatenate([turned] * 4, axis=0)
        window = kv[i, pl.ds(start, 32), :].astype(F32)
        inside = (row32 >= off) & (row32 < off + 8)
        kv[i, pl.ds(start, 32), :] = jnp.where(inside, turned, window).astype(BF)
        q = qs[pl.ds(pl.multiple_of(32 * slot, 32), 32), :].astype(BF)
        score = lax.dot_general(q, kv[i], NT, preferred_element_type=F32) * (1.0 / math.sqrt(HD))
        score = jnp.where(reach <= first, score, -1e30)
        e = jnp.exp(score - jnp.max(score, axis=1, keepdims=True))
        weight = e / jnp.sum(e, axis=1, keepdims=True)
        weight = pltpu.roll(weight, 1, 1).astype(BF)
        return jnp.dot(weight, kv[i], preferred_element_type=F32)

    def block(b, carry):
        pltpu.make_async_copy(kv_hbm.at[pl.ds(8 * b, 8)], kv.at[pl.ds(8 * b, 8)], sem.at[b]).wait()
        for r in range(8):
            i = 8 * b + r
            tok = ts[pl.ds(pl.multiple_of(8 * i, 8), 8), :]
            os[pl.ds(pl.multiple_of(32 * i, 32), 32), :] = one(i, i, scal[i], tok)
        return carry

    lax.fori_loop(0, 8, block, 0)

    for s in range(STEPS):
        for j in range(MIG):
            a = MIG * s + j
            kv[REQ + a] = arrived[s][j, 0:KV, :]
            tails[...] = arrived[s][j, KV:MSG, :].astype(F32)
            slot = scal[REQ + a]
            tok = ts[pl.ds(pl.multiple_of(8 * slot, 8), 8), :]
            for t in range(s):
                g = TOK + GHOSTS.index((s, j, t))
                tok = jnp.where(row8 == 2 * t, tails[24 + 2 * t : 25 + 2 * t, :], tok)
                new = tails[25 + 2 * t : 26 + 2 * t, :] + dv[g : g + 1, :]
                tok = jnp.where(row8 == 2 * t + 1, new, tok)
            mixed = one(REQ + a, slot, scal[REQ + STEPS * MIG + a], tok)
            keep = 8 * s
            os[pl.ds(pl.multiple_of(32 * slot + keep, 8), 32 - keep), :] = mixed[keep:, :]

    for t in range(STEPS):
        for h in range(HEADS):
            out[REQ * t : REQ * t + REQ, HD * h : HD * h + HD] = os[
                pl.ds(8 * t + h, REQ, stride=32), :
            ].astype(BF)


def local(
    hidden, query_base, kv_base, kv_cache, cache_lengths, adapter_ids, migrating, pair_mask,
    owners, pool_down, pool_upq, pool_upv, store_down, store_upq, store_upv,
):
    reps = lax.axis_size("rep")
    core = lax.axis_index("rep") % 2
    same_core = [[r for r in range(reps) if r % 2 == k] for k in range(2)]
    other_core = [(r, r ^ 1) for r in range(reps)]
    n = STEPS * MIG
    kv = kv_cache.reshape(REQ, KV, HD)
    x = hidden.reshape(TOK, D)
    kvb = kv_base.reshape(STEPS * 2 * REQ, HD)
    slots = migrating.reshape(n)

    packed = call(
        pack_kernel, "pack", jax.ShapeDtypeStruct((32, PIECE, 128), BF), [VM] * 3, nbytes=900000
    )(store_down.reshape(128, D), store_upq.reshape(RANK, D), store_upv.reshape(RANK, HD))
    got = lax.all_to_all(packed, "rep", 0, 0, tiled=True)
    copies = call(
        pick_kernel, "pick", jax.ShapeDtypeStruct((16, STEPS, PIECE, 128), BF), [SM, VM], nbytes=1400000
    )(owners, got)
    own = lax.all_to_all(copies, "rep", 0, 0, tiled=True, axis_index_groups=same_core)
    oth = lax.ppermute(own, "rep", other_core)

    meta = jnp.concatenate([cache_lengths[:, None], adapter_ids[: STEPS - 1].T], axis=1).astype(BF)
    meta = jnp.pad(meta, ((0, 0), (0, 128 - STEPS)))
    mine = call(
        message_kernel,
        "message",
        jax.ShapeDtypeStruct((n, MSG, 128), BF),
        [SM, ANY, VM, VM, VM],
        [pltpu.VMEM((32 * n, 128), F32), pltpu.SemaphoreType.DMA((n,))],
        nbytes=1700000,
    )(slots, kv, x, kvb, meta)
    row = lax.broadcasted_iota(jnp.int32, (MSG, 128), 0)
    lane = lax.broadcasted_iota(jnp.int32, (MSG, 128), 1)
    step_of = jnp.where(row < KV + 24, (row - KV) // 8, (row - KV - 24) // 2)
    step_of = jnp.where(row < KV, -1, step_of)
    step_of = jnp.where(row == KV + 30, lane - 1, step_of)
    exchange = [
        (lambda v, bit=bit: lax.ppermute(v, "rep", [(r, r ^ (1 << bit)) for r in range(reps)]))
        for bit in range(reps.bit_length() - 1)
    ]
    arrived = []
    for s in range(STEPS):
        sent = mine[MIG * s : MIG * s + MIG]
        for e in range(s):
            for j in range(MIG):
                same = migrating[s] == migrating[e, j]
                take = same[:, None, None] & (step_of < e)[None]
                sent = jnp.where(take, arrived[e][j][None], sent)
        which = sum((pair_mask[s] >= (2 << b)).astype(jnp.int32) for b in range(len(exchange) - 1))
        arrived.append(lax.switch(which, exchange, sent))
    tags = jnp.stack([a[:, KV + 30, :STEPS] for a in arrived]).astype(jnp.int32)
    ghost_ids = jnp.stack([tags[s, j, 1 + t] for s, j, t in GHOSTS])
    ids = jnp.concatenate([adapter_ids.reshape(TOK), jnp.pad(ghost_ids, (0, GHOST - len(GHOSTS)))])
    ids = jnp.broadcast_to(ids[:, None], (ROWS, 128))
    scal = jnp.concatenate([cache_lengths, slots, tags[:, :, 0].reshape(n), core[None].astype(jnp.int32)])

    parts = call(
        project_kernel,
        "project",
        jax.ShapeDtypeStruct((8, ROWS, 128), BF),
        [SM] + [VM] * 8,
        [pltpu.VMEM((SLOTS * 128, D), BF), pltpu.VMEM((ROWS, D), BF), pltpu.VMEM((GHOST, D), F32)],
        flops=2 * ROWS * D * SLOTS * 128,
        nbytes=4000000,
    )(core[None].astype(jnp.int32), x, *arrived[1:], ids, pool_down.reshape(POOL * 128, D), own, oth)
    parts = lax.all_to_all(parts, "tp", 0, 0, tiled=True)

    out = call(
        attend_kernel,
        "attend",
        jax.ShapeDtypeStruct((TOK, D), BF),
        [SM] + [VM] * 8 + [ANY] + [VM] * 4,
        [
            pltpu.VMEM((REQ + n, KV, HD), BF),
            pltpu.VMEM((SLOTS * 128, D), BF),
            pltpu.VMEM((SLOTS * 128, HD), BF),
            pltpu.VMEM((REQ * 32, HD), F32),
            pltpu.VMEM((REQ * 32, HD), F32),
            pltpu.VMEM((REQ * 8, HD), F32),
            pltpu.VMEM((STEPS * 2 * REQ, HD), F32),
            pltpu.VMEM((ROWS, HD), F32),
            pltpu.VMEM((32, HD), F32),
            pltpu.SemaphoreType.DMA((8,)),
        ],
        flops=2 * 72 * 32 * 256 * 128 * 2,
        nbytes=9000000,
    )(
        scal, parts, ids, pool_upq.reshape(POOL * RANK, D), pool_upv.reshape(POOL * RANK, HD),
        own, oth, query_base.reshape(TOK, D), kvb, kv, *arrived,
    )
    return out.reshape(STEPS, REQ, D)


def solution(mesh):
    return jax.shard_map(
        local,
        mesh=mesh,
        in_specs=(
            P(None, "rep", "tp"),
            P(None, "rep", "tp"),
            P(None, "rep", None, "tp"),
            P("rep", None, None, "tp"),
            P("rep"),
            P(None, "rep"),
            P(None, "rep"),
            P(),
            P(),
            P(None, None, None, "tp"),
            P(None, None, "tp"),
            P(None, None, "tp"),
            P("rep", None, None, "tp"),
            P("rep", None, "tp"),
            P("rep", None, "tp"),
        ),
        out_specs=P(None, "rep", "tp"),
        check_vma=False,
    )
```

```python
import functools
import math

import jax
import jax.numpy as jnp
from jax import lax
from jax.experimental import pallas as pl
from jax.experimental.pallas import tpu as pltpu
from jax.sharding import PartitionSpec as P

STEPS = 4
MIG = 2
POOL = 2
SLOTS = POOL + STEPS
REQ = 64
CTX = 128
HD = 128
HEADS = 8
D = 1024
RANK = 64
TOK = STEPS * REQ
GHOST = 16
ROWS = TOK + GHOST
MSG = 288
KV = 2 * CTX
PIECE = 56
F32 = jnp.float32
BF = jnp.bfloat16
NT = (((1,), (1,)), ((), ()))


VM = pl.BlockSpec(memory_space=pltpu.VMEM)
SM = pl.BlockSpec(memory_space=pltpu.SMEM)
ANY = pl.BlockSpec(memory_space=pl.ANY)

GHOSTS = [(s, j, t) for s in range(1, STEPS) for j in range(MIG) for t in range(s)]


def call(kernel, name, out_shape, in_specs, scratch=(), flops=0, nbytes=0):
    return pl.pallas_call(
        kernel,
        name=name,
        out_shape=out_shape,
        in_specs=in_specs,
        out_specs=VM,
        scratch_shapes=list(scratch),
        cost_estimate=pl.CostEstimate(flops=flops, bytes_accessed=nbytes, transcendentals=0),
    )


def pack_kernel(down, upq, upv, out):
    for k in range(2):
        for p in range(16):
            g, b = p // 4, p % 4
            j = (p // 8) * 16 + (p % 8) * 2 + k
            cols = slice(512 * k + 128 * b, 512 * k + 128 * b + 128)
            out[j, 0:32, :] = down[32 * g : 32 * g + 32, cols]
            out[j, 32:48, :] = upq[16 * g : 16 * g + 16, cols]
            out[j, 48:56, :] = upv[8 * (p % 8) : 8 * (p % 8) + 8, :]


def pick_kernel(owners, got, out):
    for s in range(STEPS):
        piece = got[owners[s]]
        for p in range(16):
            out[p, s] = piece


def message_kernel(slots, lens, adapters, kv_hbm, hidden, kvb, out, tail, sem):
    copies = [
        pltpu.make_async_copy(kv_hbm.at[slots[m]], out.at[m, pl.ds(0, KV)], sem.at[m])
        for m in range(STEPS * MIG)
    ]
    for copy in copies:
        copy.start()
    n = STEPS * MIG
    row = lax.broadcasted_iota(jnp.int32, (n, 128), 0)
    lane = lax.broadcasted_iota(jnp.int32, (n, 128), 1)
    slot = jnp.zeros((n, 128), jnp.int32)
    for m in range(n):
        slot = jnp.where(row == m, slots[m], slot)
    one = jnp.where(lane == slot, 1.0, 0.0).astype(BF)[:, :REQ]
    key = jnp.where(lane == 2 * slot, 1.0, 0.0).astype(BF)
    val = jnp.where(lane == 2 * slot + 1, 1.0, 0.0).astype(BF)
    for t in range(STEPS - 1):
        picked = jnp.dot(one, hidden[REQ * t : REQ * t + REQ, :], preferred_element_type=F32)
        for b in range(8):
            tail[pl.ds(8 * t + b, n, stride=32), :] = picked[:, 128 * b : 128 * b + 128]
        base = kvb[128 * t : 128 * t + 128, :]
        tail[pl.ds(24 + 2 * t, n, stride=32), :] = jnp.dot(key, base, preferred_element_type=F32)
        tail[pl.ds(25 + 2 * t, n, stride=32), :] = jnp.dot(val, base, preferred_element_type=F32)
    tags = jnp.zeros((n, 128), jnp.int32)
    for m in range(n):
        tags = jnp.where((row == m) & (lane == 0), lens[slots[m]], tags)
        for t in range(STEPS - 1):
            tags = jnp.where((row == m) & (lane == 1 + t), adapters[t, slots[m]], tags)
    tail[pl.ds(30, n, stride=32), :] = tags.astype(F32)
    tail[pl.ds(31, n, stride=32), :] = jnp.zeros((n, 128), F32)
    for m in range(n):
        out[m, KV:MSG, :] = tail[32 * m : 32 * m + 32, :].astype(BF)
    for copy in copies:
        copy.wait()


def ghost_ids(arrived, gid):
    gid[...] = jnp.zeros_like(gid)
    for g, (s, j, t) in enumerate(GHOSTS):
        tag = arrived[s][j, KV + 16 : KV + 32, :].astype(F32)[14:15, 1 + t : 2 + t]
        gid[g : g + 1, :] = jnp.broadcast_to(tag, (1, 128)).astype(jnp.int32)


def resolve_kernel(step, slots, mine, *refs):
    earlier, out = refs[:-1], refs[-1]
    row = lax.broadcasted_iota(jnp.int32, (32, 128), 0)
    lane = lax.broadcasted_iota(jnp.int32, (32, 128), 1)
    made = jnp.where(row < 24, row // 8, (row - 24) // 2)
    made = jnp.where(row == 30, lane - 1, made)
    out[...] = mine[...]
    for e in range(step):
        for i in range(MIG):
            for j in range(MIG):

                @pl.when(slots[MIG * step + j] == slots[MIG * e + i])
                def _(e=e, i=i, j=j):
                    out[j, 0:KV, :] = earlier[e][i, 0:KV, :]
                    old = out[j, KV:MSG, :].astype(F32)
                    came = earlier[e][i, KV:MSG, :].astype(F32)
                    out[j, KV:MSG, :] = jnp.where(made < e, came, old).astype(BF)


def project_kernel(core, hidden, arr1, arr2, arr3, ids, pool, own, oth, out, w, x, gx, gid):
    w[0 : POOL * 128, :] = pool[...]
    mine = core[0] * 512
    theirs = 512 - mine
    for s in range(STEPS):
        for p in range(16):
            g, b = p // 4, p % 4
            rows = slice((POOL + s) * 128 + 32 * g, (POOL + s) * 128 + 32 * g + 32)
            w[rows, pl.ds(pl.multiple_of(mine + 128 * b, 128), 128)] = own[p, s, 0:32, :]
            w[rows, pl.ds(pl.multiple_of(theirs + 128 * b, 128), 128)] = oth[p, s, 0:32, :]
    x[0:TOK, :] = hidden[...]
    gx[...] = jnp.zeros_like(gx)
    arrived = (None, arr1, arr2, arr3)
    for g, (s, j, t) in enumerate(GHOSTS):
        history = arrived[s][j, KV : KV + 32, :].astype(F32)
        for b in range(8):
            gx[g : g + 1, 128 * b : 128 * b + 128] = history[8 * t + b : 8 * t + b + 1, :]
    x[TOK:ROWS, :] = gx[...].astype(BF)
    ghost_ids(arrived, gid)
    total = jnp.zeros((TOK, 128), F32)
    ghost = jnp.zeros((GHOST, 128), F32)
    for a in range(SLOTS):
        part = lax.dot_general(x[...], w[128 * a : 128 * a + 128, :], NT, preferred_element_type=F32)
        total = jnp.where(ids[...] == a, part[:TOK], total)
        ghost = jnp.where(gid[...] == a, part[TOK:], ghost)
    total = jnp.concatenate([total, ghost], axis=0).astype(BF)
    for c in range(8):
        out[c] = total


def attend_kernel(
    lens, slots, core, parts, ids, pool_q, pool_v, own, oth, qb, kvb, kv_hbm, arr0, arr1, arr2, arr3,
    out, kv, ws, wq, wv, qs, os, ts, base, dv, tails, gid, sem,
):
    copies = [
        pltpu.make_async_copy(kv_hbm.at[pl.ds(8 * b, 8)], kv.at[pl.ds(8 * b, 8)], sem.at[b])
        for b in range(8)
    ]
    for copy in copies:
        copy.start()
    arrived = (arr0, arr1, arr2, arr3)

    mine = core[0] * 512
    theirs = 512 - mine
    for a in range(SLOTS):
        wq[128 * a + RANK : 128 * a + 128, :] = jnp.zeros((RANK, D), BF)
        wv[128 * a : 128 * a + RANK, :] = jnp.zeros((RANK, HD), BF)
    for a in range(POOL):
        wq[128 * a : 128 * a + RANK, :] = pool_q[RANK * a : RANK * a + RANK, :]
        wv[128 * a + RANK : 128 * a + 128, :] = pool_v[RANK * a : RANK * a + RANK, :]
    for s in range(STEPS):
        top = 128 * (POOL + s)
        for p in range(16):
            g, b = p // 4, p % 4
            rows = slice(top + 16 * g, top + 16 * g + 16)
            wq[rows, pl.ds(pl.multiple_of(mine + 128 * b, 128), 128)] = own[p, s, 32:48, :]
            wq[rows, pl.ds(pl.multiple_of(theirs + 128 * b, 128), 128)] = oth[p, s, 32:48, :]
        for p in range(8):
            wv[top + RANK + 8 * p : top + RANK + 8 * p + 8, :] = own[p, s, 48:56, :]

    u = parts[0].astype(F32)
    for c in range(1, 8):
        u = u + parts[c].astype(F32)
    ghost_ids(arrived, gid)
    local_u, ghost_u = u[:TOK], u[TOK:]
    spread = jnp.concatenate(
        [
            jnp.concatenate(
                [jnp.where(ids[...] == a, local_u, 0.0), jnp.where(gid[...] == a, ghost_u, 0.0)], axis=0
            ).astype(BF)
            for a in range(SLOTS)
        ],
        axis=1,
    )
    dv[...] = jnp.dot(spread, wv[...], preferred_element_type=F32)
    dq = jnp.dot(spread[:TOK], wq[...], preferred_element_type=F32)
    base[...] = kvb[...].astype(F32)
    for t in range(STEPS):
        for h in range(HEADS):
            cols = slice(HD * h, HD * h + HD)
            query = qb[REQ * t : REQ * t + REQ, cols].astype(F32) + dq[REQ * t : REQ * t + REQ, cols]
            qs[pl.ds(8 * t + h, REQ, stride=32), :] = query
        ts[pl.ds(2 * t, REQ, stride=8), :] = base[pl.ds(128 * t, REQ, stride=2), :]
        ts[pl.ds(2 * t + 1, REQ, stride=8), :] = (
            base[pl.ds(128 * t + 1, REQ, stride=2), :] + dv[REQ * t : REQ * t + REQ, :]
        )

    col = lax.broadcasted_iota(jnp.int32, (32, KV), 1)
    step_of = lax.broadcasted_iota(jnp.int32, (32, KV), 0) // HEADS
    reach = jnp.where(col % 2 == 0, col - 2 * step_of, 4 * KV)
    row32 = lax.broadcasted_iota(jnp.int32, (32, HD), 0)
    row8 = lax.broadcasted_iota(jnp.int32, (8, HD), 0)

    def weigh(i, slot, length, tok):
        first = 2 * length
        start = pl.multiple_of(jnp.minimum((first // 16) * 16, KV - 32), 16)
        off = first - start
        turned = pltpu.roll(tok, off % 8, 0)
        turned = jnp.concatenate([turned] * 4, axis=0)
        window = kv[i, pl.ds(start, 32), :].astype(F32)
        inside = (row32 >= off) & (row32 < off + 8)
        kv[i, pl.ds(start, 32), :] = jnp.where(inside, turned, window).astype(BF)
        q = qs[pl.ds(pl.multiple_of(32 * slot, 32), 32), :].astype(BF)
        score = lax.dot_general(q, kv[i], NT, preferred_element_type=F32) * (1.0 / math.sqrt(HD))
        score = jnp.where(reach <= first, score, -1e30)
        e = jnp.exp(score - jnp.max(score, axis=1, keepdims=True))
        weight = e * (1.0 / jnp.sum(e, axis=1, keepdims=True))
        ws[i] = pltpu.roll(weight, 1, 1).astype(BF)

    def weigh_block(b, carry):
        pltpu.make_async_copy(kv_hbm.at[pl.ds(8 * b, 8)], kv.at[pl.ds(8 * b, 8)], sem.at[b]).wait()
        for r in range(8):
            i = 8 * b + r
            weigh(i, i, lens[i], ts[pl.ds(pl.multiple_of(8 * i, 8), 8), :])
        return carry

    def mix_block(b, carry):
        for r in range(8):
            i = 8 * b + r
            mixed = jnp.dot(ws[i], kv[i], preferred_element_type=F32)
            os[pl.ds(pl.multiple_of(32 * i, 32), 32), :] = mixed
        return carry

    lax.fori_loop(0, 8, weigh_block, 0)
    for s in range(STEPS):
        for j in range(MIG):
            a = MIG * s + j
            kv[REQ + a] = arrived[s][j, 0:KV, :]
            tails[...] = arrived[s][j, KV:MSG, :].astype(F32)
            slot = slots[a]
            tok = ts[pl.ds(pl.multiple_of(8 * slot, 8), 8), :]
            for t in range(s):
                g = TOK + GHOSTS.index((s, j, t))
                tok = jnp.where(row8 == 2 * t, tails[24 + 2 * t : 25 + 2 * t, :], tok)
                new = tails[25 + 2 * t : 26 + 2 * t, :] + dv[g : g + 1, :]
                tok = jnp.where(row8 == 2 * t + 1, new, tok)
            length = jnp.max(tails[30:31, 0:1]).astype(jnp.int32)
            weigh(REQ + a, slot, length, tok)
    lax.fori_loop(0, 8, mix_block, 0)
    for s in range(STEPS):
        for j in range(MIG):
            a = MIG * s + j
            keep = HEADS * s
            mixed = jnp.dot(ws[REQ + a], kv[REQ + a], preferred_element_type=F32)
            rows = pl.ds(pl.multiple_of(32 * slots[a] + keep, 8), 32 - keep)
            os[rows, :] = mixed[keep:, :]

    for t in range(STEPS):
        for h in range(HEADS):
            out[REQ * t : REQ * t + REQ, HD * h : HD * h + HD] = os[
                pl.ds(8 * t + h, REQ, stride=32), :
            ].astype(BF)


def local(
    hidden, query_base, kv_base, kv_cache, cache_lengths, adapter_ids, migrating, pair_mask,
    owners, pool_down, pool_upq, pool_upv, store_down, store_upq, store_upv,
):
    reps = lax.axis_size("rep")
    core = jnp.bitwise_and(lax.axis_index("rep"), 1)
    same_core = [[r for r in range(reps) if r % 2 == k] for k in range(2)]
    other_core = [(r, r ^ 1) for r in range(reps)]
    n = STEPS * MIG
    kv = kv_cache.reshape(REQ, KV, HD)
    x = hidden.reshape(TOK, D)
    kvb = kv_base.reshape(STEPS * 2 * REQ, HD)
    slots = migrating.reshape(n)

    core = core[None].astype(jnp.int32)
    ids = jnp.broadcast_to(adapter_ids.reshape(TOK)[:, None], (TOK, 128))
    which = sum((pair_mask >= (2 << b)).astype(jnp.int32) for b in range(reps.bit_length() - 2))

    packed = call(
        pack_kernel, "pack", jax.ShapeDtypeStruct((32, PIECE, 128), BF), [VM] * 3, nbytes=900000
    )(store_down.reshape(128, D), store_upq.reshape(RANK, D), store_upv.reshape(RANK, HD))
    got = lax.all_to_all(packed, "rep", 0, 0, tiled=True)

    mine = call(
        message_kernel,
        "message",
        jax.ShapeDtypeStruct((n, MSG, 128), BF),
        [SM, SM, SM, ANY, VM, VM],
        [pltpu.VMEM((32 * n, 128), F32), pltpu.SemaphoreType.DMA((n,))],
        nbytes=1700000,
    )(slots, cache_lengths, adapter_ids, kv, x, kvb)
    exchange = [
        (lambda v, bit=bit: lax.ppermute(v, "rep", [(r, r ^ (1 << bit)) for r in range(reps)]))
        for bit in range(reps.bit_length() - 1)
    ]
    arrived = []

    def migrate(s):
        sent = pl.pallas_call(
            functools.partial(resolve_kernel, s),
            name="resolve%d" % s,
            grid=(1,),
            out_shape=jax.ShapeDtypeStruct((MIG, MSG, 128), BF),
            in_specs=[SM, pl.BlockSpec((MIG, MSG, 128), lambda i: (s, 0, 0))] + [VM] * s,
            out_specs=pl.BlockSpec((MIG, MSG, 128), lambda i: (0, 0, 0)),
            cost_estimate=pl.CostEstimate(flops=0, bytes_accessed=300000, transcendentals=0),
        )(slots, mine, *arrived)
        arrived.append(lax.switch(which[s], exchange, sent))

    migrate(0)
    migrate(1)
    got, arrived[0], arrived[1] = lax.optimization_barrier((got, arrived[0], arrived[1]))
    copies = call(
        pick_kernel, "pick", jax.ShapeDtypeStruct((16, STEPS, PIECE, 128), BF), [SM, VM], nbytes=1400000
    )(owners, got)
    own = lax.all_to_all(copies, "rep", 0, 0, tiled=True, axis_index_groups=same_core)
    migrate(2)
    migrate(3)
    own, arrived[2], arrived[3] = lax.optimization_barrier((own, arrived[2], arrived[3]))
    oth = lax.ppermute(own, "rep", other_core)

    parts = call(
        project_kernel,
        "project",
        jax.ShapeDtypeStruct((8, ROWS, 128), BF),
        [SM] + [VM] * 8,
        [
            pltpu.VMEM((SLOTS * 128, D), BF),
            pltpu.VMEM((ROWS, D), BF),
            pltpu.VMEM((GHOST, D), F32),
            pltpu.VMEM((GHOST, 128), jnp.int32),
        ],
        flops=2 * ROWS * D * SLOTS * 128,
        nbytes=4000000,
    )(core, x, *arrived[1:], ids, pool_down.reshape(POOL * 128, D), own, oth)
    parts = lax.all_to_all(parts, "tp", 0, 0, tiled=True)

    out = call(
        attend_kernel,
        "attend",
        jax.ShapeDtypeStruct((TOK, D), BF),
        [SM] * 3 + [VM] * 8 + [ANY] + [VM] * 4,
        [
            pltpu.VMEM((REQ + n, KV, HD), BF),
            pltpu.VMEM((REQ + n, 32, KV), BF),
            pltpu.VMEM((SLOTS * 128, D), BF),
            pltpu.VMEM((SLOTS * 128, HD), BF),
            pltpu.VMEM((REQ * 32, HD), F32),
            pltpu.VMEM((REQ * 32, HD), F32),
            pltpu.VMEM((REQ * 8, HD), F32),
            pltpu.VMEM((STEPS * 2 * REQ, HD), F32),
            pltpu.VMEM((ROWS, HD), F32),
            pltpu.VMEM((32, HD), F32),
            pltpu.VMEM((GHOST, 128), jnp.int32),
            pltpu.SemaphoreType.DMA((8,)),
        ],
        flops=2 * 72 * 32 * 256 * 128 * 2,
        nbytes=9000000,
    )(
        cache_lengths, slots, core, parts, ids, pool_upq.reshape(POOL * RANK, D),
        pool_upv.reshape(POOL * RANK, HD), own, oth, query_base.reshape(TOK, D), kvb, kv, *arrived,
    )
    return out.reshape(STEPS, REQ, D)


def solution(mesh):
    return jax.shard_map(
        local,
        mesh=mesh,
        in_specs=(
            P(None, "rep", "tp"),
            P(None, "rep", "tp"),
            P(None, "rep", None, "tp"),
            P("rep", None, None, "tp"),
            P("rep"),
            P(None, "rep"),
            P(None, "rep"),
            P(),
            P(),
            P(None, None, None, "tp"),
            P(None, None, "tp"),
            P(None, None, "tp"),
            P("rep", None, None, "tp"),
            P("rep", None, "tp"),
            P("rep", None, "tp"),
        ),
        out_specs=P(None, "rep", "tp"),
        check_vma=False,
    )
```

```python
import functools
import math

import jax
import jax.numpy as jnp
from jax import lax
from jax.experimental import pallas as pl
from jax.experimental.pallas import tpu as pltpu
from jax.sharding import PartitionSpec as P

STEPS = 4
MIG = 2
POOL = 2
SLOTS = POOL + STEPS
REQ = 64
CTX = 128
HD = 128
HEADS = 8
D = 1024
RANK = 64
TOK = STEPS * REQ
GHOST = 16
ROWS = TOK + GHOST
MSG = 288
KV = 2 * CTX
PIECE = 56
F32 = jnp.float32
BF = jnp.bfloat16
NT = (((1,), (1,)), ((), ()))


VM = pl.BlockSpec(memory_space=pltpu.VMEM)
SM = pl.BlockSpec(memory_space=pltpu.SMEM)
HBM = pl.BlockSpec(memory_space=pltpu.HBM)

GHOSTS = [(s, j, t) for s in range(1, STEPS) for j in range(MIG) for t in range(s)]


def call(kernel, name, out_shape, in_specs, scratch=(), flops=0, nbytes=0, out_specs=VM, mib=16):
    return pl.pallas_call(
        kernel,
        name=name,
        out_shape=out_shape,
        in_specs=in_specs,
        out_specs=out_specs,
        scratch_shapes=list(scratch),
        cost_estimate=pl.CostEstimate(flops=flops, bytes_accessed=nbytes, transcendentals=0),
        compiler_params=pltpu.CompilerParams(vmem_limit_bytes=mib << 20),
    )


def pack_kernel(down, upq, upv, out):
    for k in range(2):
        for p in range(16):
            g, b = p // 4, p % 4
            j = (p // 8) * 16 + (p % 8) * 2 + k
            cols = slice(512 * k + 128 * b, 512 * k + 128 * b + 128)
            out[j, 0:32, :] = down[32 * g : 32 * g + 32, cols]
            out[j, 32:48, :] = upq[16 * g : 16 * g + 16, cols]
            out[j, 48:56, :] = upv[8 * (p % 8) : 8 * (p % 8) + 8, :]


def pick_kernel(owners, got, out):
    for s in range(STEPS):
        piece = got[owners[s]]
        for p in range(16):
            out[p, s] = piece


def message_kernel(slots, lens, masks, adapters, kv_hbm, hidden, kvb, adapters_v, out, ids, *rest):
    which, (tail, sem) = rest[:STEPS], rest[STEPS:]
    n = STEPS * MIG
    slot_of = [slots[m % MIG, m // MIG] for m in range(n)]
    copies = [
        pltpu.make_async_copy(kv_hbm.at[slot_of[m]], out.at[m, pl.ds(0, KV)], sem.at[m]) for m in range(n)
    ]
    for copy in copies:
        copy.start()
    for s in range(STEPS):
        mask = masks[s]
        which[s][0] = sum((mask >= (2 << b)).astype(jnp.int32) for b in range(4))
    row = lax.broadcasted_iota(jnp.int32, (n, 128), 0)
    lane = lax.broadcasted_iota(jnp.int32, (n, 128), 1)
    slot = jnp.zeros((n, 128), jnp.int32)
    for m in range(n):
        slot = jnp.where(row == m, slot_of[m], slot)
    one = jnp.where(lane == slot, 1.0, 0.0).astype(BF)[:, :REQ]
    key = jnp.where(lane == 2 * slot, 1.0, 0.0).astype(BF)
    val = jnp.where(lane == 2 * slot + 1, 1.0, 0.0).astype(BF)
    tags = jnp.zeros((n, 128), jnp.int32)
    for m in range(n):
        tags = jnp.where((row == m) & (lane == 0), lens[slot_of[m]], tags)
        for t in range(STEPS - 1):
            tags = jnp.where((row == m) & (lane == 1 + t), adapters[t, slot_of[m]], tags)
    for t in range(STEPS - 1):
        picked = jnp.dot(one, hidden[REQ * t : REQ * t + REQ, :], preferred_element_type=F32)
        for b in range(8):
            tail[pl.ds(8 * t + b, n, stride=32), :] = picked[:, 128 * b : 128 * b + 128]
        base = kvb[128 * t : 128 * t + 128, :]
        tail[pl.ds(24 + 2 * t, n, stride=32), :] = jnp.dot(key, base, preferred_element_type=F32)
        tail[pl.ds(25 + 2 * t, n, stride=32), :] = jnp.dot(val, base, preferred_element_type=F32)
    tail[pl.ds(30, n, stride=32), :] = tags.astype(F32)
    tail[pl.ds(31, n, stride=32), :] = jnp.zeros((n, 128), F32)
    for m in range(n):
        out[m, KV:MSG, :] = tail[32 * m : 32 * m + 32, :].astype(BF)
    down_row = lax.broadcasted_iota(jnp.int32, (REQ, REQ), 0)
    across = lax.broadcasted_iota(jnp.int32, (REQ, REQ), 1)
    for t in range(STEPS):
        spread = jnp.where(down_row == across, adapters_v[t : t + 1, :].astype(F32), 0.0)
        column = jnp.sum(spread, axis=1, keepdims=True)
        ids[REQ * t : REQ * t + REQ, :] = jnp.broadcast_to(column, (REQ, 128)).astype(jnp.int32)
    for copy in copies:
        copy.wait()


def carry_over(slots, step, tails, cache, old, came):
    row = lax.broadcasted_iota(jnp.int32, (32, 128), 0)
    lane = lax.broadcasted_iota(jnp.int32, (32, 128), 1)
    made = jnp.where(row < 24, row // 8, (row - 24) // 2)
    made = jnp.where(row == 30, lane - 1, made)
    for e in range(step):
        for i in range(MIG):
            for j in range(MIG):

                @pl.when(slots[j, step] == slots[i, e])
                def _(e=e, i=i, j=j):
                    if cache:
                        old[j, 0:KV, :] = came[e][0][i, 0:KV, :]
                    if tails:
                        mine = old[j, -32:, :].astype(F32)
                        theirs = came[e][1][i, -32:, :].astype(F32)
                        old[j, -32:, :] = jnp.where(made < e, theirs, mine).astype(BF)


def resolve_kernel(step, tails, cache, slots, mine, *refs):
    out = refs[-1]
    out[...] = mine[...]
    carry_over(slots, step, tails, cache, out, [(r, r) for r in refs[:-1]])


def own_kernel(core, hidden, arr1, tail2, tail3, ids, pool, own, acc, x, all_ids, w, gx):
    mine = pl.multiple_of(core[0] * 512, 512)
    for s in range(STEPS):
        for p in range(16):
            g, b = p // 4, p % 4
            w[128 * s + 32 * g : 128 * s + 32 * g + 32, 128 * b : 128 * b + 128] = own[p, s, 0:32, :]
    x[0:TOK, :] = hidden[...]
    all_ids[0:TOK, :] = ids[...]
    all_ids[TOK:ROWS, :] = jnp.zeros((GHOST, 128), jnp.int32)
    gx[...] = jnp.zeros_like(gx)
    arrived = (None, arr1, tail2, tail3)
    for g, (s, j, t) in enumerate(GHOSTS):
        history = arrived[s][j, -32:, :].astype(F32)
        for b in range(8):
            gx[g : g + 1, 128 * b : 128 * b + 128] = history[8 * t + b : 8 * t + b + 1, :]
        tag = jnp.broadcast_to(history[30:31, 1 + t : 2 + t], (1, 128))
        all_ids[TOK + g : TOK + g + 1, :] = tag.astype(jnp.int32)
    x[TOK:ROWS, :] = gx[...].astype(BF)
    total = jnp.zeros((ROWS, 128), F32)
    for a in range(POOL):
        part = lax.dot_general(x[...], pool[128 * a : 128 * a + 128, :], NT, preferred_element_type=F32)
        total = jnp.where(all_ids[...] == a, part, total)
    for s in range(STEPS):
        part = lax.dot_general(
            x[:, pl.ds(mine, 512)], w[128 * s : 128 * s + 128, :], NT, preferred_element_type=F32
        )
        total = jnp.where(all_ids[...] == POOL + s, part, total)
    acc[...] = total


def other_kernel(core, acc, x, all_ids, oth, out, w):
    theirs = pl.multiple_of(512 - core[0] * 512, 512)
    for s in range(STEPS):
        for p in range(16):
            g, b = p // 4, p % 4
            w[128 * s + 32 * g : 128 * s + 32 * g + 32, 128 * b : 128 * b + 128] = oth[p, s, 0:32, :]
    more = jnp.zeros((ROWS, 128), F32)
    for s in range(STEPS):
        part = lax.dot_general(
            x[:, pl.ds(theirs, 512)], w[128 * s : 128 * s + 128, :], NT, preferred_element_type=F32
        )
        more = jnp.where(all_ids[...] == POOL + s, part, more)
    total = (acc[...] + more).astype(BF)
    for c in range(8):
        out[c] = total


def attend_kernel(
    lens, slots, core, parts, ids, pool_q, pool_v, own, oth, qb, kvb, kv_hbm, arr0, arr1, kv2, kv3, tail2, tail3,
    out, kv, ws, wq, wv, qs, os, ts, base, dv, tails, sem,
):
    copies = [
        pltpu.make_async_copy(kv_hbm.at[pl.ds(8 * b, 8)], kv.at[pl.ds(8 * b, 8)], sem.at[b])
        for b in range(8)
    ]
    for copy in copies:
        copy.start()
    arrived = (arr0, arr1, kv2, kv3)
    history = (arr0, arr1, tail2, tail3)

    mine = core[0] * 512
    theirs = 512 - mine
    for a in range(SLOTS):
        wq[128 * a + RANK : 128 * a + 128, :] = jnp.zeros((RANK, D), BF)
        wv[128 * a : 128 * a + RANK, :] = jnp.zeros((RANK, HD), BF)
    for a in range(POOL):
        wq[128 * a : 128 * a + RANK, :] = pool_q[RANK * a : RANK * a + RANK, :]
        wv[128 * a + RANK : 128 * a + 128, :] = pool_v[RANK * a : RANK * a + RANK, :]
    for s in range(STEPS):
        top = 128 * (POOL + s)
        for p in range(16):
            g, b = p // 4, p % 4
            rows = slice(top + 16 * g, top + 16 * g + 16)
            wq[rows, pl.ds(pl.multiple_of(mine + 128 * b, 128), 128)] = own[p, s, 32:48, :]
            wq[rows, pl.ds(pl.multiple_of(theirs + 128 * b, 128), 128)] = oth[p, s, 32:48, :]
        for p in range(8):
            wv[top + RANK + 8 * p : top + RANK + 8 * p + 8, :] = own[p, s, 48:56, :]

    u = parts[0].astype(F32)
    for c in range(1, 8):
        u = u + parts[c].astype(F32)
    spread = jnp.concatenate([jnp.where(ids[...] == a, u, 0.0).astype(BF) for a in range(SLOTS)], axis=1)
    dv[...] = jnp.dot(spread, wv[...], preferred_element_type=F32)
    dq = jnp.dot(spread[:TOK], wq[...], preferred_element_type=F32)
    base[...] = kvb[...].astype(F32)
    for t in range(STEPS):
        for h in range(HEADS):
            cols = slice(HD * h, HD * h + HD)
            query = qb[REQ * t : REQ * t + REQ, cols].astype(F32) + dq[REQ * t : REQ * t + REQ, cols]
            qs[pl.ds(8 * t + h, REQ, stride=32), :] = query
        ts[pl.ds(2 * t, REQ, stride=8), :] = base[pl.ds(128 * t, REQ, stride=2), :]
        ts[pl.ds(2 * t + 1, REQ, stride=8), :] = (
            base[pl.ds(128 * t + 1, REQ, stride=2), :] + dv[REQ * t : REQ * t + REQ, :]
        )

    col = lax.broadcasted_iota(jnp.int32, (32, KV), 1)
    step_of = lax.broadcasted_iota(jnp.int32, (32, KV), 0) // HEADS
    reach = jnp.where(col % 2 == 0, col - 2 * step_of, 4 * KV)
    row32 = lax.broadcasted_iota(jnp.int32, (32, HD), 0)
    row8 = lax.broadcasted_iota(jnp.int32, (8, HD), 0)

    def weigh(i, slot, length, tok):
        first = 2 * length
        start = pl.multiple_of(jnp.minimum((first // 16) * 16, KV - 32), 16)
        off = first - start
        turned = pltpu.roll(tok, off % 8, 0)
        turned = jnp.concatenate([turned] * 4, axis=0)
        window = kv[i, pl.ds(start, 32), :].astype(F32)
        inside = (row32 >= off) & (row32 < off + 8)
        kv[i, pl.ds(start, 32), :] = jnp.where(inside, turned, window).astype(BF)
        q = qs[pl.ds(pl.multiple_of(32 * slot, 32), 32), :].astype(BF)
        score = lax.dot_general(q, kv[i], NT, preferred_element_type=F32) * (1.0 / math.sqrt(HD))
        score = jnp.where(reach <= first, score, -1e30)
        e = jnp.exp(score - jnp.max(score, axis=1, keepdims=True))
        weight = e * (1.0 / jnp.sum(e, axis=1, keepdims=True))
        ws[i] = pltpu.roll(weight, 1, 1).astype(BF)

    def weigh_block(b, carry):
        pltpu.make_async_copy(kv_hbm.at[pl.ds(8 * b, 8)], kv.at[pl.ds(8 * b, 8)], sem.at[b]).wait()
        for r in range(8):
            i = 8 * b + r
            weigh(i, i, lens[i], ts[pl.ds(pl.multiple_of(8 * i, 8), 8), :])
        return carry

    def mix_block(b, carry):
        for r in range(8):
            i = 8 * b + r
            mixed = jnp.dot(ws[i], kv[i], preferred_element_type=F32)
            os[pl.ds(pl.multiple_of(32 * i, 32), 32), :] = mixed
        return carry

    lax.fori_loop(0, 8, weigh_block, 0)
    for s in range(STEPS):
        for j in range(MIG):
            a = MIG * s + j
            kv[REQ + a] = arrived[s][j, 0:KV, :]
            tails[...] = history[s][j, -32:, :].astype(F32)
            slot = slots[j, s]
            tok = ts[pl.ds(pl.multiple_of(8 * slot, 8), 8), :]
            for t in range(s):
                g = TOK + GHOSTS.index((s, j, t))
                tok = jnp.where(row8 == 2 * t, tails[24 + 2 * t : 25 + 2 * t, :], tok)
                new = tails[25 + 2 * t : 26 + 2 * t, :] + dv[g : g + 1, :]
                tok = jnp.where(row8 == 2 * t + 1, new, tok)
            length = jnp.max(tails[30:31, 0:1]).astype(jnp.int32)
            weigh(REQ + a, slot, length, tok)
    lax.fori_loop(0, 8, mix_block, 0)
    for s in range(STEPS):
        for j in range(MIG):
            a = MIG * s + j
            keep = HEADS * s
            mixed = jnp.dot(ws[REQ + a], kv[REQ + a], preferred_element_type=F32)
            rows = pl.ds(pl.multiple_of(32 * slots[j, s] + keep, 8), 32 - keep)
            os[rows, :] = mixed[keep:, :]

    for t in range(STEPS):
        for h in range(HEADS):
            out[REQ * t : REQ * t + REQ, HD * h : HD * h + HD] = os[
                pl.ds(8 * t + h, REQ, stride=32), :
            ].astype(BF)


def local(
    hidden, query_base, kv_base, kv_cache, cache_lengths, adapter_ids, migrating, pair_mask,
    owners, pool_down, pool_upq, pool_upv, store_down, store_upq, store_upv,
):
    reps = lax.axis_size("rep")
    core = jnp.bitwise_and(lax.axis_index("rep"), 1)
    same_core = [[r for r in range(reps) if r % 2 == k] for k in range(2)]
    other_core = [(r, r ^ 1) for r in range(reps)]
    n = STEPS * MIG
    kv = kv_cache.reshape(REQ, KV, HD)
    x = hidden.reshape(TOK, D)
    kvb = kv_base.reshape(STEPS * 2 * REQ, HD)
    slots = migrating.T

    core = core[None].astype(jnp.int32)

    packed = call(
        pack_kernel, "pack", jax.ShapeDtypeStruct((32, PIECE, 128), BF), [VM] * 3, nbytes=900000
    )(store_down.reshape(128, D), store_upq.reshape(RANK, D), store_upv.reshape(RANK, HD))
    got = lax.all_to_all(packed, "rep", 0, 0, tiled=True)

    mine, ids, *which = call(
        message_kernel,
        "message",
        [jax.ShapeDtypeStruct((n, MSG, 128), BF), jax.ShapeDtypeStruct((TOK, 128), jnp.int32)]
        + [jax.ShapeDtypeStruct((1,), jnp.int32)] * STEPS,
        [SM] * 4 + [HBM] + [VM] * 3,
        [pltpu.VMEM((32 * n, 128), F32), pltpu.SemaphoreType.DMA((n,))],
        nbytes=1700000,
        out_specs=[VM, VM] + [SM] * STEPS,
    )(slots, cache_lengths, pair_mask, adapter_ids, kv, x, kvb, adapter_ids)
    exchange = [
        (lambda v, bit=bit: lax.ppermute(v, "rep", [(r, r ^ (1 << bit)) for r in range(reps)]))
        for bit in range(reps.bit_length() - 1)
    ]

    def migrate(s, rows, block, tails, cache, mine, came):
        sent = pl.pallas_call(
            functools.partial(resolve_kernel, s, tails, cache),
            name="resolve%d" % s,
            grid=(1,),
            out_shape=jax.ShapeDtypeStruct((MIG, rows, 128), BF),
            in_specs=[SM, pl.BlockSpec((MIG, rows, 128), lambda i: (s, block, 0))] + [VM] * s,
            out_specs=pl.BlockSpec((MIG, rows, 128), lambda i: (0, 0, 0)),
            cost_estimate=pl.CostEstimate(flops=0, bytes_accessed=300000, transcendentals=0),
            compiler_params=pltpu.CompilerParams(vmem_limit_bytes=8 << 20),
        )(slots, mine, *came)
        return lax.switch(which[s][0], exchange, sent)

    arr0 = migrate(0, MSG, 0, True, True, mine, [])
    arr1 = migrate(1, MSG, 0, True, True, mine, [arr0])
    got, arr0, arr1 = lax.optimization_barrier((got, arr0, arr1))
    copies = call(
        pick_kernel, "pick", jax.ShapeDtypeStruct((16, STEPS, PIECE, 128), BF), [SM, VM], nbytes=1400000
    )(owners, got)
    own = lax.all_to_all(copies, "rep", 0, 0, tiled=True, axis_index_groups=same_core)
    tail2 = migrate(2, 32, 8, True, False, mine, [arr0, arr1])
    tail3 = migrate(3, 32, 8, True, False, mine, [arr0, arr1, tail2])
    own, tail2, tail3 = lax.optimization_barrier((own, tail2, tail3))
    oth = lax.ppermute(own, "rep", other_core)

    acc, tokens, all_ids = call(
        own_kernel,
        "project_own",
        [
            jax.ShapeDtypeStruct((ROWS, 128), F32),
            jax.ShapeDtypeStruct((ROWS, D), BF),
            jax.ShapeDtypeStruct((ROWS, 128), jnp.int32),
        ],
        [SM] + [VM] * 7,
        [pltpu.VMEM((STEPS * 128, D // 2), BF), pltpu.VMEM((GHOST, D), F32)],
        flops=ROWS * D * SLOTS * 128,
        nbytes=4000000,
        out_specs=[VM] * 3,
    )(core, x, arr1, tail2, tail3, ids, pool_down.reshape(POOL * 128, D), own)
    parts = call(
        other_kernel,
        "project_other",
        jax.ShapeDtypeStruct((8, ROWS, 128), BF),
        [SM] + [VM] * 4,
        [pltpu.VMEM((STEPS * 128, D // 2), BF)],
        flops=ROWS * D * SLOTS * 128,
        nbytes=2000000,
    )(core, acc, tokens, all_ids, oth)
    parts, mine = lax.optimization_barrier((parts, mine))
    parts = lax.all_to_all(parts, "tp", 0, 0, tiled=True)
    kv2 = migrate(2, KV, 0, False, True, mine, [arr0, arr1])
    kv3 = migrate(3, KV, 0, False, True, mine, [arr0, arr1, kv2])
    parts, kv2, kv3 = lax.optimization_barrier((parts, kv2, kv3))

    out = call(
        attend_kernel,
        "attend",
        jax.ShapeDtypeStruct((TOK, D), BF),
        [SM] * 3 + [VM] * 8 + [HBM] + [VM] * 6,
        [
            pltpu.VMEM((REQ + n, KV, HD), BF),
            pltpu.VMEM((REQ + n, 32, KV), BF),
            pltpu.VMEM((SLOTS * 128, D), BF),
            pltpu.VMEM((SLOTS * 128, HD), BF),
            pltpu.VMEM((REQ * 32, HD), F32),
            pltpu.VMEM((REQ * 32, HD), F32),
            pltpu.VMEM((REQ * 8, HD), F32),
            pltpu.VMEM((STEPS * 2 * REQ, HD), F32),
            pltpu.VMEM((ROWS, HD), F32),
            pltpu.VMEM((32, HD), F32),
            pltpu.SemaphoreType.DMA((8,)),
        ],
        flops=2 * 72 * 32 * 256 * 128 * 2,
        nbytes=9000000,
        mib=32,
    )(
        cache_lengths, slots, core, parts, all_ids, pool_upq.reshape(POOL * RANK, D),
        pool_upv.reshape(POOL * RANK, HD), own, oth, query_base.reshape(TOK, D), kvb, kv,
        arr0, arr1, kv2, kv3, tail2, tail3,
    )
    return out.reshape(STEPS, REQ, D)


def solution(mesh):
    return jax.shard_map(
        local,
        mesh=mesh,
        in_specs=(
            P(None, "rep", "tp"),
            P(None, "rep", "tp"),
            P(None, "rep", None, "tp"),
            P("rep", None, None, "tp"),
            P("rep"),
            P(None, "rep"),
            P(None, "rep"),
            P(),
            P(),
            P(None, None, None, "tp"),
            P(None, None, "tp"),
            P(None, None, "tp"),
            P("rep", None, None, "tp"),
            P("rep", None, "tp"),
            P("rep", None, "tp"),
        ),
        out_specs=P(None, "rep", "tp"),
        check_vma=False,
    )
```

```python
import functools
import math

import jax
import jax.numpy as jnp
from jax import lax
from jax.experimental import pallas as pl
from jax.experimental.pallas import tpu as pltpu
from jax.sharding import PartitionSpec as P

STEPS = 4
MIG = 2
POOL = 2
SLOTS = POOL + STEPS
REQ = 64
CTX = 128
HD = 128
HEADS = 8
D = 1024
RANK = 64
TOK = STEPS * REQ
GHOST = 16
ROWS = TOK + GHOST
MSG = 288
KV = 2 * CTX
PIECE = 56
F32 = jnp.float32
BF = jnp.bfloat16
NT = (((1,), (1,)), ((), ()))


VM = pl.BlockSpec(memory_space=pltpu.VMEM)
SM = pl.BlockSpec(memory_space=pltpu.SMEM)
HBM = pl.BlockSpec(memory_space=pltpu.HBM)

GHOSTS = [(s, j, t) for s in range(1, STEPS) for j in range(MIG) for t in range(s)]


def call(kernel, name, out_shape, in_specs, scratch=(), flops=0, nbytes=0, out_specs=VM, mib=None):
    return pl.pallas_call(
        kernel,
        name=name,
        out_shape=out_shape,
        in_specs=in_specs,
        out_specs=out_specs,
        scratch_shapes=list(scratch),
        cost_estimate=pl.CostEstimate(flops=flops, bytes_accessed=nbytes, transcendentals=0),
        compiler_params=pltpu.CompilerParams(vmem_limit_bytes=mib and mib << 20),
    )


def pack_kernel(down, upq, upv, out):
    for k in range(2):
        for p in range(16):
            g, b = p // 4, p % 4
            j = (p // 8) * 16 + (p % 8) * 2 + k
            cols = slice(512 * k + 128 * b, 512 * k + 128 * b + 128)
            out[j, 0:32, :] = down[32 * g : 32 * g + 32, cols]
            out[j, 32:48, :] = upq[16 * g : 16 * g + 16, cols]
            out[j, 48:56, :] = upv[8 * (p % 8) : 8 * (p % 8) + 8, :]


def pick_kernel(owners, got, out):
    for s in range(STEPS):
        piece = got[owners[s]]
        for p in range(16):
            out[p, s] = piece


def message_kernel(slots, lens, masks, adapters, kv_hbm, hidden, kvb, adapters_v, out, ids, *rest):
    which, (tail, sem) = rest[:STEPS], rest[STEPS:]
    n = STEPS * MIG
    slot_of = [slots[m % MIG, m // MIG] for m in range(n)]
    copies = [
        pltpu.make_async_copy(kv_hbm.at[slot_of[m]], out.at[m, pl.ds(0, KV)], sem.at[m]) for m in range(n)
    ]
    for copy in copies:
        copy.start()
    for s in range(STEPS):
        mask = masks[s]
        which[s][0] = sum((mask >= (2 << b)).astype(jnp.int32) for b in range(4))
    row = lax.broadcasted_iota(jnp.int32, (n, 128), 0)
    lane = lax.broadcasted_iota(jnp.int32, (n, 128), 1)
    slot = jnp.zeros((n, 128), jnp.int32)
    for m in range(n):
        slot = jnp.where(row == m, slot_of[m], slot)
    one = jnp.where(lane == slot, 1.0, 0.0).astype(BF)[:, :REQ]
    key = jnp.where(lane == 2 * slot, 1.0, 0.0).astype(BF)
    val = jnp.where(lane == 2 * slot + 1, 1.0, 0.0).astype(BF)
    tags = jnp.zeros((n, 128), jnp.int32)
    for m in range(n):
        tags = jnp.where((row == m) & (lane == 0), lens[slot_of[m]], tags)
        for t in range(STEPS - 1):
            tags = jnp.where((row == m) & (lane == 1 + t), adapters[t, slot_of[m]], tags)
    for t in range(STEPS - 1):
        picked = jnp.dot(one, hidden[REQ * t : REQ * t + REQ, :], preferred_element_type=F32)
        for b in range(8):
            tail[pl.ds(8 * t + b, n, stride=32), :] = picked[:, 128 * b : 128 * b + 128]
        base = kvb[128 * t : 128 * t + 128, :]
        tail[pl.ds(24 + 2 * t, n, stride=32), :] = jnp.dot(key, base, preferred_element_type=F32)
        tail[pl.ds(25 + 2 * t, n, stride=32), :] = jnp.dot(val, base, preferred_element_type=F32)
    tail[pl.ds(30, n, stride=32), :] = tags.astype(F32)
    tail[pl.ds(31, n, stride=32), :] = jnp.zeros((n, 128), F32)
    for m in range(n):
        out[m, KV:MSG, :] = tail[32 * m : 32 * m + 32, :].astype(BF)
    down_row = lax.broadcasted_iota(jnp.int32, (REQ, REQ), 0)
    across = lax.broadcasted_iota(jnp.int32, (REQ, REQ), 1)
    for t in range(STEPS):
        spread = jnp.where(down_row == across, adapters_v[t : t + 1, :].astype(F32), 0.0)
        column = jnp.sum(spread, axis=1, keepdims=True)
        ids[REQ * t : REQ * t + REQ, :] = jnp.broadcast_to(column, (REQ, 128)).astype(jnp.int32)
    for copy in copies:
        copy.wait()


def resolve_kernel(step, slots, mine, *refs):
    earlier, out = refs[:-1], refs[-1]
    row = lax.broadcasted_iota(jnp.int32, (32, 128), 0)
    lane = lax.broadcasted_iota(jnp.int32, (32, 128), 1)
    made = jnp.where(row < 24, row // 8, (row - 24) // 2)
    made = jnp.where(row == 30, lane - 1, made)
    out[...] = mine[...]
    for e in range(step):
        for i in range(MIG):
            for j in range(MIG):

                @pl.when(slots[j, step] == slots[i, e])
                def _(e=e, i=i, j=j):
                    out[j, 0:KV, :] = earlier[e][i, 0:KV, :]
                    old = out[j, KV:MSG, :].astype(F32)
                    came = earlier[e][i, KV:MSG, :].astype(F32)
                    out[j, KV:MSG, :] = jnp.where(made < e, came, old).astype(BF)


def own_kernel(core, hidden, arr1, arr2, arr3, ids, pool_hbm, own, acc, x, all_ids, w, gx, pool, sem):
    copies = [
        pltpu.make_async_copy(hidden, x.at[pl.ds(0, TOK)], sem.at[0]),
        pltpu.make_async_copy(ids, all_ids.at[pl.ds(0, TOK)], sem.at[1]),
        pltpu.make_async_copy(pool_hbm, pool, sem.at[2]),
    ]
    for copy in copies:
        copy.start()
    mine = pl.multiple_of(core[0] * 512, 512)
    for s in range(STEPS):
        for p in range(16):
            g, b = p // 4, p % 4
            w[128 * s + 32 * g : 128 * s + 32 * g + 32, 128 * b : 128 * b + 128] = own[p, s, 0:32, :]
    all_ids[TOK:ROWS, :] = jnp.zeros((GHOST, 128), jnp.int32)
    gx[...] = jnp.zeros_like(gx)
    arrived = (None, arr1, arr2, arr3)
    for g, (s, j, t) in enumerate(GHOSTS):
        history = arrived[s][j, -32:, :].astype(F32)
        for b in range(8):
            gx[g : g + 1, 128 * b : 128 * b + 128] = history[8 * t + b : 8 * t + b + 1, :]
        tag = jnp.broadcast_to(history[30:31, 1 + t : 2 + t], (1, 128))
        all_ids[TOK + g : TOK + g + 1, :] = tag.astype(jnp.int32)
    x[TOK:ROWS, :] = gx[...].astype(BF)
    for copy in copies:
        copy.wait()
    total = jnp.zeros((ROWS, 128), F32)
    for a in range(POOL):
        part = lax.dot_general(x[...], pool[128 * a : 128 * a + 128, :], NT, preferred_element_type=F32)
        total = jnp.where(all_ids[...] == a, part, total)
    for s in range(STEPS):
        part = lax.dot_general(
            x[:, pl.ds(mine, 512)], w[128 * s : 128 * s + 128, :], NT, preferred_element_type=F32
        )
        total = jnp.where(all_ids[...] == POOL + s, part, total)
    acc[...] = total


def other_kernel(core, acc, x, all_ids, oth, out, w):
    theirs = pl.multiple_of(512 - core[0] * 512, 512)
    for s in range(STEPS):
        for p in range(16):
            g, b = p // 4, p % 4
            w[128 * s + 32 * g : 128 * s + 32 * g + 32, 128 * b : 128 * b + 128] = oth[p, s, 0:32, :]
    more = jnp.zeros((ROWS, 128), F32)
    for s in range(STEPS):
        part = lax.dot_general(
            x[:, pl.ds(theirs, 512)], w[128 * s : 128 * s + 128, :], NT, preferred_element_type=F32
        )
        more = jnp.where(all_ids[...] == POOL + s, part, more)
    total = (acc[...] + more).astype(BF)
    for c in range(8):
        out[c] = total


def attend_kernel(
    lens, slots, core, parts, ids, pool_q, pool_v, own, oth, qb, kvb, kv_hbm, arr0, arr1, arr2, arr3,
    out, kv, ws, wq, wv, qs, os, ts, base, dv, tails, sem,
):
    copies = [
        pltpu.make_async_copy(kv_hbm.at[pl.ds(8 * b, 8)], kv.at[pl.ds(8 * b, 8)], sem.at[b])
        for b in range(8)
    ]
    for copy in copies:
        copy.start()
    arrived = (arr0, arr1, arr2, arr3)

    mine = core[0] * 512
    theirs = 512 - mine
    for a in range(SLOTS):
        wq[128 * a + RANK : 128 * a + 128, :] = jnp.zeros((RANK, D), BF)
        wv[128 * a : 128 * a + RANK, :] = jnp.zeros((RANK, HD), BF)
    for a in range(POOL):
        wq[128 * a : 128 * a + RANK, :] = pool_q[RANK * a : RANK * a + RANK, :]
        wv[128 * a + RANK : 128 * a + 128, :] = pool_v[RANK * a : RANK * a + RANK, :]
    for s in range(STEPS):
        top = 128 * (POOL + s)
        for p in range(16):
            g, b = p // 4, p % 4
            rows = slice(top + 16 * g, top + 16 * g + 16)
            wq[rows, pl.ds(pl.multiple_of(mine + 128 * b, 128), 128)] = own[p, s, 32:48, :]
            wq[rows, pl.ds(pl.multiple_of(theirs + 128 * b, 128), 128)] = oth[p, s, 32:48, :]
        for p in range(8):
            wv[top + RANK + 8 * p : top + RANK + 8 * p + 8, :] = own[p, s, 48:56, :]

    u = parts[0].astype(F32)
    for c in range(1, 8):
        u = u + parts[c].astype(F32)
    spread = jnp.concatenate([jnp.where(ids[...] == a, u, 0.0).astype(BF) for a in range(SLOTS)], axis=1)
    dv[...] = jnp.dot(spread, wv[...], preferred_element_type=F32)
    dq = jnp.dot(spread[:TOK], wq[...], preferred_element_type=F32)
    base[...] = kvb[...].astype(F32)
    for t in range(STEPS):
        for h in range(HEADS):
            cols = slice(HD * h, HD * h + HD)
            query = qb[REQ * t : REQ * t + REQ, cols].astype(F32) + dq[REQ * t : REQ * t + REQ, cols]
            qs[pl.ds(8 * t + h, REQ, stride=32), :] = query
        ts[pl.ds(2 * t, REQ, stride=8), :] = base[pl.ds(128 * t, REQ, stride=2), :]
        ts[pl.ds(2 * t + 1, REQ, stride=8), :] = (
            base[pl.ds(128 * t + 1, REQ, stride=2), :] + dv[REQ * t : REQ * t + REQ, :]
        )

    col = lax.broadcasted_iota(jnp.int32, (32, KV), 1)
    step_of = lax.broadcasted_iota(jnp.int32, (32, KV), 0) // HEADS
    reach = jnp.where(col % 2 == 0, col - 2 * step_of, 4 * KV)
    row32 = lax.broadcasted_iota(jnp.int32, (32, HD), 0)
    row8 = lax.broadcasted_iota(jnp.int32, (8, HD), 0)

    def weigh(i, slot, length, tok):
        first = 2 * length
        start = pl.multiple_of(jnp.minimum((first // 16) * 16, KV - 32), 16)
        off = first - start
        turned = pltpu.roll(tok, off % 8, 0)
        turned = jnp.concatenate([turned] * 4, axis=0)
        window = kv[i, pl.ds(start, 32), :].astype(F32)
        inside = (row32 >= off) & (row32 < off + 8)
        kv[i, pl.ds(start, 32), :] = jnp.where(inside, turned, window).astype(BF)
        q = qs[pl.ds(pl.multiple_of(32 * slot, 32), 32), :].astype(BF)
        score = lax.dot_general(q, kv[i], NT, preferred_element_type=F32) * (1.0 / math.sqrt(HD))
        score = jnp.where(reach <= first, score, -1e30)
        e = jnp.exp(score - jnp.max(score, axis=1, keepdims=True))
        weight = e * (1.0 / jnp.sum(e, axis=1, keepdims=True))
        ws[i] = pltpu.roll(weight, 1, 1).astype(BF)

    def weigh_block(b, carry):
        pltpu.make_async_copy(kv_hbm.at[pl.ds(8 * b, 8)], kv.at[pl.ds(8 * b, 8)], sem.at[b]).wait()
        for r in range(8):
            i = 8 * b + r
            weigh(i, i, lens[i], ts[pl.ds(pl.multiple_of(8 * i, 8), 8), :])
        return carry

    def mix_block(b, carry):
        for r in range(8):
            i = 8 * b + r
            mixed = jnp.dot(ws[i], kv[i], preferred_element_type=F32)
            os[pl.ds(pl.multiple_of(32 * i, 32), 32), :] = mixed
        return carry

    lax.fori_loop(0, 8, weigh_block, 0)
    for s in range(STEPS):
        for j in range(MIG):
            a = MIG * s + j
            kv[REQ + a] = arrived[s][j, 0:KV, :]
            tails[...] = arrived[s][j, KV:MSG, :].astype(F32)
            slot = slots[j, s]
            tok = ts[pl.ds(pl.multiple_of(8 * slot, 8), 8), :]
            for t in range(s):
                g = TOK + GHOSTS.index((s, j, t))
                tok = jnp.where(row8 == 2 * t, tails[24 + 2 * t : 25 + 2 * t, :], tok)
                new = tails[25 + 2 * t : 26 + 2 * t, :] + dv[g : g + 1, :]
                tok = jnp.where(row8 == 2 * t + 1, new, tok)
            length = jnp.max(tails[30:31, 0:1]).astype(jnp.int32)
            weigh(REQ + a, slot, length, tok)
    lax.fori_loop(0, 8, mix_block, 0)
    for s in range(STEPS):
        for j in range(MIG):
            a = MIG * s + j
            keep = HEADS * s
            mixed = jnp.dot(ws[REQ + a], kv[REQ + a], preferred_element_type=F32)
            rows = pl.ds(pl.multiple_of(32 * slots[j, s] + keep, 8), 32 - keep)
            os[rows, :] = mixed[keep:, :]

    for t in range(STEPS):
        for h in range(HEADS):
            out[REQ * t : REQ * t + REQ, HD * h : HD * h + HD] = os[
                pl.ds(8 * t + h, REQ, stride=32), :
            ].astype(BF)


def local(
    hidden, query_base, kv_base, kv_cache, cache_lengths, adapter_ids, migrating, pair_mask,
    owners, pool_down, pool_upq, pool_upv, store_down, store_upq, store_upv,
):
    reps = lax.axis_size("rep")
    core = jnp.bitwise_and(lax.axis_index("rep"), 1)
    same_core = [[r for r in range(reps) if r % 2 == k] for k in range(2)]
    other_core = [(r, r ^ 1) for r in range(reps)]
    n = STEPS * MIG
    kv = kv_cache.reshape(REQ, KV, HD)
    x = hidden.reshape(TOK, D)
    kvb = kv_base.reshape(STEPS * 2 * REQ, HD)
    slots = migrating.T

    core = core[None].astype(jnp.int32)

    packed = call(
        pack_kernel, "pack", jax.ShapeDtypeStruct((32, PIECE, 128), BF), [VM] * 3, nbytes=900000
    )(store_down.reshape(128, D), store_upq.reshape(RANK, D), store_upv.reshape(RANK, HD))
    got = lax.all_to_all(packed, "rep", 0, 0, tiled=True)

    mine, ids, *which = call(
        message_kernel,
        "message",
        [jax.ShapeDtypeStruct((n, MSG, 128), BF), jax.ShapeDtypeStruct((TOK, 128), jnp.int32)]
        + [jax.ShapeDtypeStruct((1,), jnp.int32)] * STEPS,
        [SM] * 4 + [HBM] + [VM] * 3,
        [pltpu.VMEM((32 * n, 128), F32), pltpu.SemaphoreType.DMA((n,))],
        nbytes=1700000,
        out_specs=[VM, VM] + [SM] * STEPS,
    )(slots, cache_lengths, pair_mask, adapter_ids, kv, x, kvb, adapter_ids)
    exchange = [
        (lambda v, bit=bit: lax.ppermute(v, "rep", [(r, r ^ (1 << bit)) for r in range(reps)]))
        for bit in range(reps.bit_length() - 1)
    ]

    def migrate(s, came):
        sent = pl.pallas_call(
            functools.partial(resolve_kernel, s),
            name="resolve%d" % s,
            grid=(1,),
            out_shape=jax.ShapeDtypeStruct((MIG, MSG, 128), BF),
            in_specs=[SM, pl.BlockSpec((MIG, MSG, 128), lambda i: (s, 0, 0))] + [VM] * s,
            out_specs=pl.BlockSpec((MIG, MSG, 128), lambda i: (0, 0, 0)),
            cost_estimate=pl.CostEstimate(flops=0, bytes_accessed=300000, transcendentals=0),
        )(slots, mine, *came)
        return lax.switch(which[s][0], exchange, sent)

    arr0 = migrate(0, [])
    arr1 = migrate(1, [arr0])
    got, arr0, arr1 = lax.optimization_barrier((got, arr0, arr1))
    copies = call(
        pick_kernel, "pick", jax.ShapeDtypeStruct((16, STEPS, PIECE, 128), BF), [SM, VM], nbytes=1400000, mib=8
    )(owners, got)
    own = lax.all_to_all(copies, "rep", 0, 0, tiled=True, axis_index_groups=same_core)
    arr2 = migrate(2, [arr0, arr1])
    arr3 = migrate(3, [arr0, arr1, arr2])
    own, arr2, arr3 = lax.optimization_barrier((own, arr2, arr3))
    oth = lax.ppermute(own, "rep", other_core)

    acc, tokens, all_ids = call(
        own_kernel,
        "project_own",
        [
            jax.ShapeDtypeStruct((ROWS, 128), F32),
            jax.ShapeDtypeStruct((ROWS, D), BF),
            jax.ShapeDtypeStruct((ROWS, 128), jnp.int32),
        ],
        [SM, HBM] + [VM] * 3 + [HBM, HBM, VM],
        [
            pltpu.VMEM((STEPS * 128, D // 2), BF),
            pltpu.VMEM((GHOST, D), F32),
            pltpu.VMEM((POOL * 128, D), BF),
            pltpu.SemaphoreType.DMA((3,)),
        ],
        flops=ROWS * D * SLOTS * 128,
        nbytes=4000000,
        out_specs=[VM] * 3,
        mib=12,
    )(core, x, arr1, arr2, arr3, ids, pool_down.reshape(POOL * 128, D), own)
    parts = call(
        other_kernel,
        "project_other",
        jax.ShapeDtypeStruct((8, ROWS, 128), BF),
        [SM] + [VM] * 4,
        [pltpu.VMEM((STEPS * 128, D // 2), BF)],
        flops=ROWS * D * SLOTS * 128,
        nbytes=2000000,
        mib=8,
    )(core, acc, tokens, all_ids, oth)
    parts = lax.all_to_all(parts, "tp", 0, 0, tiled=True)

    out = call(
        attend_kernel,
        "attend",
        jax.ShapeDtypeStruct((TOK, D), BF),
        [SM] * 3 + [VM] * 8 + [HBM] + [VM] * 4,
        [
            pltpu.VMEM((REQ + n, KV, HD), BF),
            pltpu.VMEM((REQ + n, 32, KV), BF),
            pltpu.VMEM((SLOTS * 128, D), BF),
            pltpu.VMEM((SLOTS * 128, HD), BF),
            pltpu.VMEM((REQ * 32, HD), F32),
            pltpu.VMEM((REQ * 32, HD), F32),
            pltpu.VMEM((REQ * 8, HD), F32),
            pltpu.VMEM((STEPS * 2 * REQ, HD), F32),
            pltpu.VMEM((ROWS, HD), F32),
            pltpu.VMEM((32, HD), F32),
            pltpu.SemaphoreType.DMA((8,)),
        ],
        flops=2 * 72 * 32 * 256 * 128 * 2,
        nbytes=9000000,
    )(
        cache_lengths, slots, core, parts, all_ids, pool_upq.reshape(POOL * RANK, D),
        pool_upv.reshape(POOL * RANK, HD), own, oth, query_base.reshape(TOK, D), kvb, kv,
        arr0, arr1, arr2, arr3,
    )
    return out.reshape(STEPS, REQ, D)


def solution(mesh):
    return jax.shard_map(
        local,
        mesh=mesh,
        in_specs=(
            P(None, "rep", "tp"),
            P(None, "rep", "tp"),
            P(None, "rep", None, "tp"),
            P("rep", None, None, "tp"),
            P("rep"),
            P(None, "rep"),
            P(None, "rep"),
            P(),
            P(),
            P(None, None, None, "tp"),
            P(None, None, "tp"),
            P(None, None, "tp"),
            P("rep", None, None, "tp"),
            P("rep", None, "tp"),
            P("rep", None, "tp"),
        ),
        out_specs=P(None, "rep", "tp"),
        check_vma=False,
    )
```

```python
import functools
import math

import jax
import jax.numpy as jnp
from jax import lax
from jax.experimental import pallas as pl
from jax.experimental.pallas import tpu as pltpu
from jax.sharding import PartitionSpec as P

STEPS = 4
MIG = 2
POOL = 2
SLOTS = POOL + STEPS
REQ = 64
CTX = 128
HD = 128
HEADS = 8
D = 1024
RANK = 64
TOK = STEPS * REQ
GHOST = 16
ROWS = TOK + GHOST
MSG = 288
KV = 2 * CTX
PIECE = 56
F32 = jnp.float32
BF = jnp.bfloat16
NT = (((1,), (1,)), ((), ()))


VM = pl.BlockSpec(memory_space=pltpu.VMEM)
SM = pl.BlockSpec(memory_space=pltpu.SMEM)
HBM = pl.BlockSpec(memory_space=pltpu.HBM)

GHOSTS = [(s, j, t) for s in range(1, STEPS) for j in range(MIG) for t in range(s)]


def call(kernel, name, out_shape, in_specs, scratch=(), flops=0, nbytes=0, out_specs=VM, mib=None):
    return pl.pallas_call(
        kernel,
        name=name,
        out_shape=out_shape,
        in_specs=in_specs,
        out_specs=out_specs,
        scratch_shapes=list(scratch),
        cost_estimate=pl.CostEstimate(flops=flops, bytes_accessed=nbytes, transcendentals=0),
        compiler_params=pltpu.CompilerParams(vmem_limit_bytes=mib and mib << 20),
    )


def pack_kernel(down, upq, upv, out):
    for k in range(2):
        for p in range(16):
            g, b = p // 4, p % 4
            j = (p // 8) * 16 + (p % 8) * 2 + k
            cols = slice(512 * k + 128 * b, 512 * k + 128 * b + 128)
            out[j, 0:32, :] = down[32 * g : 32 * g + 32, cols]
            out[j, 32:48, :] = upq[16 * g : 16 * g + 16, cols]
            out[j, 48:56, :] = upv[8 * (p % 8) : 8 * (p % 8) + 8, :]


def pick_kernel(owners, got, out):
    for s in range(STEPS):
        piece = got[owners[s]]
        for p in range(16):
            out[p, s] = piece


def message_kernel(slots, lens, masks, adapters, kv_hbm, hidden, kvb, adapters_v, out, ids, lead, *rest):
    which, (tail, sem) = rest[:STEPS], rest[STEPS:]
    n = STEPS * MIG
    slot_of = [slots[m % MIG, m // MIG] for m in range(n)]
    copies = [
        pltpu.make_async_copy(kv_hbm.at[slot_of[m]], out.at[m, pl.ds(0, KV)], sem.at[m]) for m in range(n)
    ]
    for copy in copies:
        copy.start()
    for s in range(STEPS):
        mask = masks[s]
        which[s][0] = sum((mask >= (2 << b)).astype(jnp.int32) for b in range(4))
    row = lax.broadcasted_iota(jnp.int32, (n, 128), 0)
    lane = lax.broadcasted_iota(jnp.int32, (n, 128), 1)
    slot = jnp.zeros((n, 128), jnp.int32)
    for m in range(n):
        slot = jnp.where(row == m, slot_of[m], slot)
    one = jnp.where(lane == slot, 1.0, 0.0).astype(BF)[:, :REQ]
    key = jnp.where(lane == 2 * slot, 1.0, 0.0).astype(BF)
    val = jnp.where(lane == 2 * slot + 1, 1.0, 0.0).astype(BF)
    tags = jnp.zeros((n, 128), jnp.int32)
    for m in range(n):
        tags = jnp.where((row == m) & (lane == 0), lens[slot_of[m]], tags)
        for t in range(STEPS - 1):
            tags = jnp.where((row == m) & (lane == 1 + t), adapters[t, slot_of[m]], tags)
    for t in range(STEPS - 1):
        picked = jnp.dot(one, hidden[REQ * t : REQ * t + REQ, :], preferred_element_type=F32)
        for b in range(8):
            tail[pl.ds(8 * t + b, n, stride=32), :] = picked[:, 128 * b : 128 * b + 128]
        base = kvb[128 * t : 128 * t + 128, :]
        tail[pl.ds(24 + 2 * t, n, stride=32), :] = jnp.dot(key, base, preferred_element_type=F32)
        tail[pl.ds(25 + 2 * t, n, stride=32), :] = jnp.dot(val, base, preferred_element_type=F32)
    tail[pl.ds(30, n, stride=32), :] = tags.astype(F32)
    tail[pl.ds(31, n, stride=32), :] = jnp.zeros((n, 128), F32)
    for m in range(n):
        out[m, KV:MSG, :] = tail[32 * m : 32 * m + 32, :].astype(BF)
    down_row = lax.broadcasted_iota(jnp.int32, (REQ, REQ), 0)
    across = lax.broadcasted_iota(jnp.int32, (REQ, REQ), 1)
    for t in range(STEPS):
        spread = jnp.where(down_row == across, adapters_v[t : t + 1, :].astype(F32), 0.0)
        column = jnp.sum(spread, axis=1, keepdims=True)
        ids[REQ * t : REQ * t + REQ, :] = jnp.broadcast_to(column, (REQ, 128)).astype(jnp.int32)
    for m in range(MIG):
        lead[m, KV:MSG, :] = tail[32 * m : 32 * m + 32, :].astype(BF)
    for copy in copies:
        copy.wait()
    for m in range(MIG):
        lead[m, 0:KV, :] = out[m, 0:KV, :]


def resolve_kernel(step, slots, mine, *refs):
    earlier, out = refs[:-1], refs[-1]
    row = lax.broadcasted_iota(jnp.int32, (32, 128), 0)
    lane = lax.broadcasted_iota(jnp.int32, (32, 128), 1)
    made = jnp.where(row < 24, row // 8, (row - 24) // 2)
    made = jnp.where(row == 30, lane - 1, made)
    out[...] = mine[...]
    for e in range(step):
        for i in range(MIG):
            for j in range(MIG):

                @pl.when(slots[j, step] == slots[i, e])
                def _(e=e, i=i, j=j):
                    out[j, 0:KV, :] = earlier[e][i, 0:KV, :]
                    old = out[j, KV:MSG, :].astype(F32)
                    came = earlier[e][i, KV:MSG, :].astype(F32)
                    out[j, KV:MSG, :] = jnp.where(made < e, came, old).astype(BF)


def own_kernel(core, hidden, arr1, arr2, arr3, ids, pool_hbm, own, acc, x, all_ids, w, gx, pool, sem):
    copies = [
        pltpu.make_async_copy(hidden, x.at[pl.ds(0, TOK)], sem.at[0]),
        pltpu.make_async_copy(ids, all_ids.at[pl.ds(0, TOK)], sem.at[1]),
        pltpu.make_async_copy(pool_hbm, pool, sem.at[2]),
    ]
    for copy in copies:
        copy.start()
    mine = pl.multiple_of(core[0] * 512, 512)
    for s in range(STEPS):
        for p in range(16):
            g, b = p // 4, p % 4
            w[128 * s + 32 * g : 128 * s + 32 * g + 32, 128 * b : 128 * b + 128] = own[p, s, 0:32, :]
    all_ids[TOK:ROWS, :] = jnp.zeros((GHOST, 128), jnp.int32)
    gx[...] = jnp.zeros_like(gx)
    arrived = (None, arr1, arr2, arr3)
    for g, (s, j, t) in enumerate(GHOSTS):
        history = arrived[s][j, -32:, :].astype(F32)
        for b in range(8):
            gx[g : g + 1, 128 * b : 128 * b + 128] = history[8 * t + b : 8 * t + b + 1, :]
        tag = jnp.broadcast_to(history[30:31, 1 + t : 2 + t], (1, 128))
        all_ids[TOK + g : TOK + g + 1, :] = tag.astype(jnp.int32)
    x[TOK:ROWS, :] = gx[...].astype(BF)
    for copy in copies:
        copy.wait()
    total = jnp.zeros((ROWS, 128), F32)
    for a in range(POOL):
        part = lax.dot_general(x[...], pool[128 * a : 128 * a + 128, :], NT, preferred_element_type=F32)
        total = jnp.where(all_ids[...] == a, part, total)
    for s in range(STEPS):
        part = lax.dot_general(
            x[:, pl.ds(mine, 512)], w[128 * s : 128 * s + 128, :], NT, preferred_element_type=F32
        )
        total = jnp.where(all_ids[...] == POOL + s, part, total)
    acc[...] = total


def other_kernel(core, acc, x, all_ids, oth, out, w):
    theirs = pl.multiple_of(512 - core[0] * 512, 512)
    for s in range(STEPS):
        for p in range(16):
            g, b = p // 4, p % 4
            w[128 * s + 32 * g : 128 * s + 32 * g + 32, 128 * b : 128 * b + 128] = oth[p, s, 0:32, :]
    more = jnp.zeros((ROWS, 128), F32)
    for s in range(STEPS):
        part = lax.dot_general(
            x[:, pl.ds(theirs, 512)], w[128 * s : 128 * s + 128, :], NT, preferred_element_type=F32
        )
        more = jnp.where(all_ids[...] == POOL + s, part, more)
    total = (acc[...] + more).astype(BF)
    for c in range(8):
        out[c] = total


def prepare_kernel(core, pool_q, pool_v, own, oth, wq, wv):
    mine = core[0] * 512
    theirs = 512 - mine
    for a in range(SLOTS):
        wq[128 * a + RANK : 128 * a + 128, :] = jnp.zeros((RANK, D), BF)
        wv[128 * a : 128 * a + RANK, :] = jnp.zeros((RANK, HD), BF)
    for a in range(POOL):
        wq[128 * a : 128 * a + RANK, :] = pool_q[RANK * a : RANK * a + RANK, :]
        wv[128 * a + RANK : 128 * a + 128, :] = pool_v[RANK * a : RANK * a + RANK, :]
    for s in range(STEPS):
        top = 128 * (POOL + s)
        for p in range(16):
            g, b = p // 4, p % 4
            rows = slice(top + 16 * g, top + 16 * g + 16)
            wq[rows, pl.ds(pl.multiple_of(mine + 128 * b, 128), 128)] = own[p, s, 32:48, :]
            wq[rows, pl.ds(pl.multiple_of(theirs + 128 * b, 128), 128)] = oth[p, s, 32:48, :]
        for p in range(8):
            wv[top + RANK + 8 * p : top + RANK + 8 * p + 8, :] = own[p, s, 48:56, :]


def attend_kernel(
    lens, slots, parts, ids, wq, wv, qb, kvb, kv_hbm, arr0, arr1, arr2, arr3,
    out, kv, ws, qs, os, ts, base, dv, tails, sem,
):
    copies = [
        pltpu.make_async_copy(kv_hbm.at[pl.ds(8 * b, 8)], kv.at[pl.ds(8 * b, 8)], sem.at[b])
        for b in range(8)
    ]
    for copy in copies:
        copy.start()
    arrived = (arr0, arr1, arr2, arr3)

    u = parts[0].astype(F32)
    for c in range(1, 8):
        u = u + parts[c].astype(F32)
    spread = jnp.concatenate([jnp.where(ids[...] == a, u, 0.0).astype(BF) for a in range(SLOTS)], axis=1)
    dv[...] = jnp.dot(spread, wv[...], preferred_element_type=F32)
    dq = jnp.dot(spread[:TOK], wq[...], preferred_element_type=F32)
    base[...] = kvb[...].astype(F32)
    for t in range(STEPS):
        for h in range(HEADS):
            cols = slice(HD * h, HD * h + HD)
            query = qb[REQ * t : REQ * t + REQ, cols].astype(F32) + dq[REQ * t : REQ * t + REQ, cols]
            qs[pl.ds(8 * t + h, REQ, stride=32), :] = query
        ts[pl.ds(2 * t, REQ, stride=8), :] = base[pl.ds(128 * t, REQ, stride=2), :]
        ts[pl.ds(2 * t + 1, REQ, stride=8), :] = (
            base[pl.ds(128 * t + 1, REQ, stride=2), :] + dv[REQ * t : REQ * t + REQ, :]
        )

    col = lax.broadcasted_iota(jnp.int32, (32, KV), 1)
    step_of = lax.broadcasted_iota(jnp.int32, (32, KV), 0) // HEADS
    reach = jnp.where(col % 2 == 0, col - 2 * step_of, 4 * KV)
    row32 = lax.broadcasted_iota(jnp.int32, (32, HD), 0)
    row8 = lax.broadcasted_iota(jnp.int32, (8, HD), 0)

    def weigh(i, slot, length, tok):
        first = 2 * length
        start = pl.multiple_of(jnp.minimum((first // 16) * 16, KV - 32), 16)
        off = first - start
        turned = pltpu.roll(tok, off % 8, 0)
        turned = jnp.concatenate([turned] * 4, axis=0)
        window = kv[i, pl.ds(start, 32), :].astype(F32)
        inside = (row32 >= off) & (row32 < off + 8)
        kv[i, pl.ds(start, 32), :] = jnp.where(inside, turned, window).astype(BF)
        q = qs[pl.ds(pl.multiple_of(32 * slot, 32), 32), :].astype(BF)
        score = lax.dot_general(q, kv[i], NT, preferred_element_type=F32) * (1.0 / math.sqrt(HD))
        score = jnp.where(reach <= first, score, -1e30)
        e = jnp.exp(score - jnp.max(score, axis=1, keepdims=True))
        weight = e * (1.0 / jnp.sum(e, axis=1, keepdims=True))
        ws[i] = pltpu.roll(weight, 1, 1).astype(BF)

    def weigh_block(b, carry):
        pltpu.make_async_copy(kv_hbm.at[pl.ds(8 * b, 8)], kv.at[pl.ds(8 * b, 8)], sem.at[b]).wait()
        for r in range(8):
            i = 8 * b + r
            weigh(i, i, lens[i], ts[pl.ds(pl.multiple_of(8 * i, 8), 8), :])
        return carry

    def mix_block(b, carry):
        for r in range(8):
            i = 8 * b + r
            mixed = jnp.dot(ws[i], kv[i], preferred_element_type=F32)
            os[pl.ds(pl.multiple_of(32 * i, 32), 32), :] = mixed
        return carry

    lax.fori_loop(0, 8, weigh_block, 0)
    for s in range(STEPS):
        for j in range(MIG):
            a = MIG * s + j
            kv[REQ + a] = arrived[s][j, 0:KV, :]
            tails[...] = arrived[s][j, KV:MSG, :].astype(F32)
            slot = slots[j, s]
            tok = ts[pl.ds(pl.multiple_of(8 * slot, 8), 8), :]
            for t in range(s):
                g = TOK + GHOSTS.index((s, j, t))
                tok = jnp.where(row8 == 2 * t, tails[24 + 2 * t : 25 + 2 * t, :], tok)
                new = tails[25 + 2 * t : 26 + 2 * t, :] + dv[g : g + 1, :]
                tok = jnp.where(row8 == 2 * t + 1, new, tok)
            length = jnp.max(tails[30:31, 0:1]).astype(jnp.int32)
            weigh(REQ + a, slot, length, tok)
    lax.fori_loop(0, 8, mix_block, 0)
    for s in range(STEPS):
        for j in range(MIG):
            a = MIG * s + j
            keep = HEADS * s
            mixed = jnp.dot(ws[REQ + a], kv[REQ + a], preferred_element_type=F32)
            rows = pl.ds(pl.multiple_of(32 * slots[j, s] + keep, 8), 32 - keep)
            os[rows, :] = mixed[keep:, :]

    for t in range(STEPS):
        for h in range(HEADS):
            out[REQ * t : REQ * t + REQ, HD * h : HD * h + HD] = os[
                pl.ds(8 * t + h, REQ, stride=32), :
            ].astype(BF)


def local(
    hidden, query_base, kv_base, kv_cache, cache_lengths, adapter_ids, migrating, pair_mask,
    owners, pool_down, pool_upq, pool_upv, store_down, store_upq, store_upv,
):
    reps = lax.axis_size("rep")
    core = jnp.bitwise_and(lax.axis_index("rep"), 1)
    same_core = [[r for r in range(reps) if r % 2 == k] for k in range(2)]
    other_core = [(r, r ^ 1) for r in range(reps)]
    n = STEPS * MIG
    kv = kv_cache.reshape(REQ, KV, HD)
    x = hidden.reshape(TOK, D)
    kvb = kv_base.reshape(STEPS * 2 * REQ, HD)
    slots = migrating.T

    core = core[None].astype(jnp.int32)

    packed = call(
        pack_kernel, "pack", jax.ShapeDtypeStruct((32, PIECE, 128), BF), [VM] * 3, nbytes=900000
    )(store_down.reshape(128, D), store_upq.reshape(RANK, D), store_upv.reshape(RANK, HD))
    got = lax.all_to_all(packed, "rep", 0, 0, tiled=True)

    mine, ids, lead, *which = call(
        message_kernel,
        "message",
        [
            jax.ShapeDtypeStruct((n, MSG, 128), BF),
            jax.ShapeDtypeStruct((TOK, 128), jnp.int32),
            jax.ShapeDtypeStruct((MIG, MSG, 128), BF),
        ]
        + [jax.ShapeDtypeStruct((1,), jnp.int32)] * STEPS,
        [SM] * 4 + [HBM] + [VM] * 3,
        [pltpu.VMEM((32 * n, 128), F32), pltpu.SemaphoreType.DMA((n,))],
        nbytes=1700000,
        out_specs=[VM] * 3 + [SM] * STEPS,
    )(slots, cache_lengths, pair_mask, adapter_ids, kv, x, kvb, adapter_ids)
    exchange = [
        (lambda v, bit=bit: lax.ppermute(v, "rep", [(r, r ^ (1 << bit)) for r in range(reps)]))
        for bit in range(reps.bit_length() - 1)
    ]

    def migrate(s, came):
        sent = pl.pallas_call(
            functools.partial(resolve_kernel, s),
            name="resolve%d" % s,
            grid=(1,),
            out_shape=jax.ShapeDtypeStruct((MIG, MSG, 128), BF),
            in_specs=[SM, pl.BlockSpec((MIG, MSG, 128), lambda i: (s, 0, 0))] + [VM] * s,
            out_specs=pl.BlockSpec((MIG, MSG, 128), lambda i: (0, 0, 0)),
            cost_estimate=pl.CostEstimate(flops=0, bytes_accessed=300000, transcendentals=0),
        )(slots, mine, *came)
        return lax.switch(which[s][0], exchange, sent)

    arr0 = lax.switch(which[0][0], exchange, lead)
    arr1 = migrate(1, [arr0])
    arr2 = migrate(2, [arr0, arr1])
    got, arr0, arr1, arr2 = lax.optimization_barrier((got, arr0, arr1, arr2))
    copies = call(
        pick_kernel, "pick", jax.ShapeDtypeStruct((16, STEPS, PIECE, 128), BF), [SM, VM], nbytes=1400000, mib=8
    )(owners, got)
    own = lax.all_to_all(copies, "rep", 0, 0, tiled=True, axis_index_groups=same_core)
    arr3 = migrate(3, [arr0, arr1, arr2])
    own, arr3 = lax.optimization_barrier((own, arr3))
    oth = lax.ppermute(own, "rep", other_core)

    acc, tokens, all_ids = call(
        own_kernel,
        "project_own",
        [
            jax.ShapeDtypeStruct((ROWS, 128), F32),
            jax.ShapeDtypeStruct((ROWS, D), BF),
            jax.ShapeDtypeStruct((ROWS, 128), jnp.int32),
        ],
        [SM, HBM] + [VM] * 3 + [HBM, HBM, VM],
        [
            pltpu.VMEM((STEPS * 128, D // 2), BF),
            pltpu.VMEM((GHOST, D), F32),
            pltpu.VMEM((POOL * 128, D), BF),
            pltpu.SemaphoreType.DMA((3,)),
        ],
        flops=ROWS * D * SLOTS * 128,
        nbytes=4000000,
        out_specs=[VM] * 3,
        mib=12,
    )(core, x, arr1, arr2, arr3, ids, pool_down.reshape(POOL * 128, D), own)
    parts = call(
        other_kernel,
        "project_other",
        jax.ShapeDtypeStruct((8, ROWS, 128), BF),
        [SM] + [VM] * 4,
        [pltpu.VMEM((STEPS * 128, D // 2), BF)],
        flops=ROWS * D * SLOTS * 128,
        nbytes=2000000,
        mib=8,
    )(core, acc, tokens, all_ids, oth)
    parts, own, oth = lax.optimization_barrier((parts, own, oth))
    parts = lax.all_to_all(parts, "tp", 0, 0, tiled=True)
    wq, wv = call(
        prepare_kernel,
        "prepare",
        [jax.ShapeDtypeStruct((SLOTS * 128, D), BF), jax.ShapeDtypeStruct((SLOTS * 128, HD), BF)],
        [SM] + [VM] * 4,
        nbytes=4000000,
        out_specs=[VM] * 2,
    )(core, pool_upq.reshape(POOL * RANK, D), pool_upv.reshape(POOL * RANK, HD), own, oth)
    parts, wq, wv = lax.optimization_barrier((parts, wq, wv))

    out = call(
        attend_kernel,
        "attend",
        jax.ShapeDtypeStruct((TOK, D), BF),
        [SM] * 2 + [VM] * 6 + [HBM] + [VM] * 4,
        [
            pltpu.VMEM((REQ + n, KV, HD), BF),
            pltpu.VMEM((REQ + n, 32, KV), BF),
            pltpu.VMEM((REQ * 32, HD), F32),
            pltpu.VMEM((REQ * 32, HD), F32),
            pltpu.VMEM((REQ * 8, HD), F32),
            pltpu.VMEM((STEPS * 2 * REQ, HD), F32),
            pltpu.VMEM((ROWS, HD), F32),
            pltpu.VMEM((32, HD), F32),
            pltpu.SemaphoreType.DMA((8,)),
        ],
        flops=2 * 72 * 32 * 256 * 128 * 2,
        nbytes=9000000,
    )(
        cache_lengths, slots, parts, all_ids, wq, wv, query_base.reshape(TOK, D), kvb, kv,
        arr0, arr1, arr2, arr3,
    )
    return out.reshape(STEPS, REQ, D)


def solution(mesh):
    return jax.shard_map(
        local,
        mesh=mesh,
        in_specs=(
            P(None, "rep", "tp"),
            P(None, "rep", "tp"),
            P(None, "rep", None, "tp"),
            P("rep", None, None, "tp"),
            P("rep"),
            P(None, "rep"),
            P(None, "rep"),
            P(),
            P(),
            P(None, None, None, "tp"),
            P(None, None, "tp"),
            P(None, None, "tp"),
            P("rep", None, None, "tp"),
            P("rep", None, "tp"),
            P("rep", None, "tp"),
        ),
        out_specs=P(None, "rep", "tp"),
        check_vma=False,
    )
```

```python
import functools
import math

import jax
import jax.numpy as jnp
from jax import lax
from jax.experimental import pallas as pl
from jax.experimental.pallas import tpu as pltpu
from jax.sharding import PartitionSpec as P

STEPS = 4
MIG = 2
POOL = 2
SLOTS = POOL + STEPS
REQ = 64
CTX = 128
HD = 128
HEADS = 8
D = 1024
RANK = 64
TOK = STEPS * REQ
GHOST = 16
ROWS = TOK + GHOST
MSG = 288
KV = 2 * CTX
PIECE = 56
F32 = jnp.float32
BF = jnp.bfloat16
NT = (((1,), (1,)), ((), ()))


VM = pl.BlockSpec(memory_space=pltpu.VMEM)
SM = pl.BlockSpec(memory_space=pltpu.SMEM)
HBM = pl.BlockSpec(memory_space=pltpu.HBM)

GHOSTS = [(s, j, t) for s in range(1, STEPS) for j in range(MIG) for t in range(s)]


def call(kernel, name, out_shape, in_specs, scratch=(), flops=0, nbytes=0, out_specs=VM, mib=None):
    return pl.pallas_call(
        kernel,
        name=name,
        out_shape=out_shape,
        in_specs=in_specs,
        out_specs=out_specs,
        scratch_shapes=list(scratch),
        cost_estimate=pl.CostEstimate(flops=flops, bytes_accessed=nbytes, transcendentals=0),
        compiler_params=pltpu.CompilerParams(vmem_limit_bytes=mib and mib << 20),
    )


def pack_kernel(down, upq, upv, out):
    values = upv[...].astype(F32)
    blank = jnp.zeros((6, HD), F32)
    for k in range(2):
        for p in range(16):
            g, b = p // 4, p % 4
            j = (p // 8) * 16 + (p % 8) * 2 + k
            cols = slice(512 * k + 128 * b, 512 * k + 128 * b + 128)
            out[j, 0:32, :] = down[32 * g : 32 * g + 32, cols]
            out[j, 32:48, :] = upq[16 * g : 16 * g + 16, cols]
            c = 2 * (16 * k + p)
            out[j, 48:56, :] = jnp.concatenate([values[c : c + 2], blank], axis=0).astype(BF)


def pick_kernel(owners, got, out):
    values = []
    for s in range(STEPS):
        piece = got[owners[s]]
        values.append(piece[48:56].astype(F32)[0:2])
        for p in range(16):
            out[p, 48 * s : 48 * s + 48, :] = piece[0:48]
    values = jnp.concatenate(values, axis=0).astype(BF)
    for p in range(16):
        out[p, 192:200, :] = values


def message_kernel(slots, lens, masks, adapters, kv_hbm, hidden, kvb, adapters_v, out, ids, lead, *rest):
    which, (tail, sem) = rest[:STEPS], rest[STEPS:]
    n = STEPS * MIG
    slot_of = [slots[m % MIG, m // MIG] for m in range(n)]
    copies = [
        pltpu.make_async_copy(kv_hbm.at[slot_of[m]], out.at[m, pl.ds(0, KV)], sem.at[m]) for m in range(n)
    ]
    for copy in copies:
        copy.start()
    for s in range(STEPS):
        mask = masks[s]
        which[s][0] = sum((mask >= (2 << b)).astype(jnp.int32) for b in range(4))
    row = lax.broadcasted_iota(jnp.int32, (n, 128), 0)
    lane = lax.broadcasted_iota(jnp.int32, (n, 128), 1)
    slot = jnp.zeros((n, 128), jnp.int32)
    for m in range(n):
        slot = jnp.where(row == m, slot_of[m], slot)
    one = jnp.where(lane == slot, 1.0, 0.0).astype(BF)[:, :REQ]
    key = jnp.where(lane == 2 * slot, 1.0, 0.0).astype(BF)
    val = jnp.where(lane == 2 * slot + 1, 1.0, 0.0).astype(BF)
    tags = jnp.zeros((n, 128), jnp.int32)
    for m in range(n):
        tags = jnp.where((row == m) & (lane == 0), lens[slot_of[m]], tags)
        for t in range(STEPS - 1):
            tags = jnp.where((row == m) & (lane == 1 + t), adapters[t, slot_of[m]], tags)
    for t in range(STEPS - 1):
        picked = jnp.dot(one, hidden[REQ * t : REQ * t + REQ, :], preferred_element_type=F32)
        for b in range(8):
            tail[pl.ds(8 * t + b, n, stride=32), :] = picked[:, 128 * b : 128 * b + 128]
        base = kvb[128 * t : 128 * t + 128, :]
        tail[pl.ds(24 + 2 * t, n, stride=32), :] = jnp.dot(key, base, preferred_element_type=F32)
        tail[pl.ds(25 + 2 * t, n, stride=32), :] = jnp.dot(val, base, preferred_element_type=F32)
    tail[pl.ds(30, n, stride=32), :] = tags.astype(F32)
    tail[pl.ds(31, n, stride=32), :] = jnp.zeros((n, 128), F32)
    for m in range(n):
        out[m, KV:MSG, :] = tail[32 * m : 32 * m + 32, :].astype(BF)
    down_row = lax.broadcasted_iota(jnp.int32, (REQ, REQ), 0)
    across = lax.broadcasted_iota(jnp.int32, (REQ, REQ), 1)
    for t in range(STEPS):
        spread = jnp.where(down_row == across, adapters_v[t : t + 1, :].astype(F32), 0.0)
        column = jnp.sum(spread, axis=1, keepdims=True)
        ids[REQ * t : REQ * t + REQ, :] = jnp.broadcast_to(column, (REQ, 128)).astype(jnp.int32)
    for m in range(MIG):
        lead[m, KV:MSG, :] = tail[32 * m : 32 * m + 32, :].astype(BF)
    for copy in copies:
        copy.wait()
    for m in range(MIG):
        lead[m, 0:KV, :] = out[m, 0:KV, :]


def resolve_kernel(step, slots, mine, *refs):
    earlier, out = refs[:-1], refs[-1]
    row = lax.broadcasted_iota(jnp.int32, (32, 128), 0)
    lane = lax.broadcasted_iota(jnp.int32, (32, 128), 1)
    made = jnp.where(row < 24, row // 8, (row - 24) // 2)
    made = jnp.where(row == 30, lane - 1, made)
    out[...] = mine[...]
    for e in range(step):
        for i in range(MIG):
            for j in range(MIG):

                @pl.when(slots[j, step] == slots[i, e])
                def _(e=e, i=i, j=j):
                    out[j, 0:KV, :] = earlier[e][i, 0:KV, :]
                    old = out[j, KV:MSG, :].astype(F32)
                    came = earlier[e][i, KV:MSG, :].astype(F32)
                    out[j, KV:MSG, :] = jnp.where(made < e, came, old).astype(BF)


def own_kernel(core, hidden, arr1, arr2, arr3, ids, pool_hbm, own, acc, x, all_ids, w, gx, pool, sem):
    copies = [
        pltpu.make_async_copy(hidden, x.at[pl.ds(0, TOK)], sem.at[0]),
        pltpu.make_async_copy(ids, all_ids.at[pl.ds(0, TOK)], sem.at[1]),
        pltpu.make_async_copy(pool_hbm, pool, sem.at[2]),
    ]
    for copy in copies:
        copy.start()
    mine = pl.multiple_of(core[0] * 512, 512)
    for s in range(STEPS):
        for p in range(16):
            g, b = p // 4, p % 4
            w[128 * s + 32 * g : 128 * s + 32 * g + 32, 128 * b : 128 * b + 128] = own[p, 48 * s : 48 * s + 32, :]
    all_ids[TOK:ROWS, :] = jnp.zeros((GHOST, 128), jnp.int32)
    gx[...] = jnp.zeros_like(gx)
    arrived = (None, arr1, arr2, arr3)
    for g, (s, j, t) in enumerate(GHOSTS):
        history = arrived[s][j, -32:, :].astype(F32)
        for b in range(8):
            gx[g : g + 1, 128 * b : 128 * b + 128] = history[8 * t + b : 8 * t + b + 1, :]
        tag = jnp.broadcast_to(history[30:31, 1 + t : 2 + t], (1, 128))
        all_ids[TOK + g : TOK + g + 1, :] = tag.astype(jnp.int32)
    x[TOK:ROWS, :] = gx[...].astype(BF)
    for copy in copies:
        copy.wait()
    total = jnp.zeros((ROWS, 128), F32)
    for a in range(POOL):
        part = lax.dot_general(x[...], pool[128 * a : 128 * a + 128, :], NT, preferred_element_type=F32)
        total = jnp.where(all_ids[...] == a, part, total)
    for s in range(STEPS):
        part = lax.dot_general(
            x[:, pl.ds(mine, 512)], w[128 * s : 128 * s + 128, :], NT, preferred_element_type=F32
        )
        total = jnp.where(all_ids[...] == POOL + s, part, total)
    acc[...] = total


def other_kernel(core, acc, x, all_ids, oth, out, w):
    theirs = pl.multiple_of(512 - core[0] * 512, 512)
    for s in range(STEPS):
        for p in range(16):
            g, b = p // 4, p % 4
            w[128 * s + 32 * g : 128 * s + 32 * g + 32, 128 * b : 128 * b + 128] = oth[p, 48 * s : 48 * s + 32, :]
    more = jnp.zeros((ROWS, 128), F32)
    for s in range(STEPS):
        part = lax.dot_general(
            x[:, pl.ds(theirs, 512)], w[128 * s : 128 * s + 128, :], NT, preferred_element_type=F32
        )
        more = jnp.where(all_ids[...] == POOL + s, part, more)
    total = (acc[...] + more).astype(BF)
    for c in range(8):
        out[c] = total


def prepare_kernel(core, pool_q, pool_v, own, oth, wq, wv, values):
    mine = core[0] * 512
    theirs = 512 - mine
    for a in range(SLOTS):
        wq[128 * a + RANK : 128 * a + 128, :] = jnp.zeros((RANK, D), BF)
        wv[128 * a : 128 * a + RANK, :] = jnp.zeros((RANK, HD), BF)
    for a in range(POOL):
        wq[128 * a : 128 * a + RANK, :] = pool_q[RANK * a : RANK * a + RANK, :]
        wv[128 * a + RANK : 128 * a + 128, :] = pool_v[RANK * a : RANK * a + RANK, :]
    for s in range(STEPS):
        top = 128 * (POOL + s)
        for p in range(16):
            g, b = p // 4, p % 4
            rows = slice(top + 16 * g, top + 16 * g + 16)
            wq[rows, pl.ds(pl.multiple_of(mine + 128 * b, 128), 128)] = own[p, 48 * s + 32 : 48 * s + 48, :]
            wq[rows, pl.ds(pl.multiple_of(theirs + 128 * b, 128), 128)] = oth[p, 48 * s + 32 : 48 * s + 48, :]
    half = 32 * core[0]
    for p in range(16):
        near = own[p, 192:200, :].astype(F32)
        far = oth[p, 192:200, :].astype(F32)
        for s in range(STEPS):
            values[pl.ds(RANK * s + half + 2 * p, 2), :] = near[2 * s : 2 * s + 2]
            values[pl.ds(RANK * s + 32 - half + 2 * p, 2), :] = far[2 * s : 2 * s + 2]
    for s in range(STEPS):
        top = 128 * (POOL + s) + RANK
        wv[top : top + RANK, :] = values[RANK * s : RANK * s + RANK, :].astype(BF)


def attend_kernel(
    lens, slots, parts, ids, wq, wv, qb, kvb, kv_hbm, arr0, arr1, arr2, arr3,
    out, kv, ws, qs, os, ts, base, dv, tails, sem,
):
    copies = [
        pltpu.make_async_copy(kv_hbm.at[pl.ds(8 * b, 8)], kv.at[pl.ds(8 * b, 8)], sem.at[b])
        for b in range(8)
    ]
    for copy in copies:
        copy.start()
    arrived = (arr0, arr1, arr2, arr3)

    u = parts[0].astype(F32)
    for c in range(1, 8):
        u = u + parts[c].astype(F32)
    spread = jnp.concatenate([jnp.where(ids[...] == a, u, 0.0).astype(BF) for a in range(SLOTS)], axis=1)
    dv[...] = jnp.dot(spread, wv[...], preferred_element_type=F32)
    dq = jnp.dot(spread[:TOK], wq[...], preferred_element_type=F32)
    base[...] = kvb[...].astype(F32)
    for t in range(STEPS):
        for h in range(HEADS):
            cols = slice(HD * h, HD * h + HD)
            query = qb[REQ * t : REQ * t + REQ, cols].astype(F32) + dq[REQ * t : REQ * t + REQ, cols]
            qs[pl.ds(8 * t + h, REQ, stride=32), :] = query
        ts[pl.ds(2 * t, REQ, stride=8), :] = base[pl.ds(128 * t, REQ, stride=2), :]
        ts[pl.ds(2 * t + 1, REQ, stride=8), :] = (
            base[pl.ds(128 * t + 1, REQ, stride=2), :] + dv[REQ * t : REQ * t + REQ, :]
        )

    col = lax.broadcasted_iota(jnp.int32, (32, KV), 1)
    step_of = lax.broadcasted_iota(jnp.int32, (32, KV), 0) // HEADS
    reach = jnp.where(col % 2 == 0, col - 2 * step_of, 4 * KV)
    row32 = lax.broadcasted_iota(jnp.int32, (32, HD), 0)
    row8 = lax.broadcasted_iota(jnp.int32, (8, HD), 0)

    def weigh(i, slot, length, tok):
        first = 2 * length
        start = pl.multiple_of(jnp.minimum((first // 16) * 16, KV - 32), 16)
        off = first - start
        turned = pltpu.roll(tok, off % 8, 0)
        turned = jnp.concatenate([turned] * 4, axis=0)
        window = kv[i, pl.ds(start, 32), :].astype(F32)
        inside = (row32 >= off) & (row32 < off + 8)
        kv[i, pl.ds(start, 32), :] = jnp.where(inside, turned, window).astype(BF)
        q = qs[pl.ds(pl.multiple_of(32 * slot, 32), 32), :].astype(BF)
        score = lax.dot_general(q, kv[i], NT, preferred_element_type=F32) * (1.0 / math.sqrt(HD))
        score = jnp.where(reach <= first, score, -1e30)
        e = jnp.exp(score - jnp.max(score, axis=1, keepdims=True))
        weight = e * (1.0 / jnp.sum(e, axis=1, keepdims=True))
        ws[i] = pltpu.roll(weight, 1, 1).astype(BF)

    def weigh_block(b, carry):
        for c in range(2):
            eight = pl.ds(16 * b + 8 * c, 8)
            pltpu.make_async_copy(kv_hbm.at[eight], kv.at[eight], sem.at[2 * b + c]).wait()
        for r in range(16):
            i = 16 * b + r
            weigh(i, i, lens[i], ts[pl.ds(pl.multiple_of(8 * i, 8), 8), :])
        return carry

    def mix_block(b, carry):
        for r in range(16):
            i = 16 * b + r
            mixed = jnp.dot(ws[i], kv[i], preferred_element_type=F32)
            os[pl.ds(pl.multiple_of(32 * i, 32), 32), :] = mixed
        return carry

    lax.fori_loop(0, 4, weigh_block, 0)
    for s in range(STEPS):
        for j in range(MIG):
            a = MIG * s + j
            kv[REQ + a] = arrived[s][j, 0:KV, :]
            tails[...] = arrived[s][j, KV:MSG, :].astype(F32)
            slot = slots[j, s]
            tok = ts[pl.ds(pl.multiple_of(8 * slot, 8), 8), :]
            for t in range(s):
                g = TOK + GHOSTS.index((s, j, t))
                tok = jnp.where(row8 == 2 * t, tails[24 + 2 * t : 25 + 2 * t, :], tok)
                new = tails[25 + 2 * t : 26 + 2 * t, :] + dv[g : g + 1, :]
                tok = jnp.where(row8 == 2 * t + 1, new, tok)
            length = jnp.max(tails[30:31, 0:1]).astype(jnp.int32)
            weigh(REQ + a, slot, length, tok)
    lax.fori_loop(0, 4, mix_block, 0)
    for s in range(STEPS):
        for j in range(MIG):
            a = MIG * s + j
            keep = HEADS * s
            mixed = jnp.dot(ws[REQ + a], kv[REQ + a], preferred_element_type=F32)
            rows = pl.ds(pl.multiple_of(32 * slots[j, s] + keep, 8), 32 - keep)
            os[rows, :] = mixed[keep:, :]

    for t in range(STEPS):
        for h in range(HEADS):
            out[REQ * t : REQ * t + REQ, HD * h : HD * h + HD] = os[
                pl.ds(8 * t + h, REQ, stride=32), :
            ].astype(BF)


def local(
    hidden, query_base, kv_base, kv_cache, cache_lengths, adapter_ids, migrating, pair_mask,
    owners, pool_down, pool_upq, pool_upv, store_down, store_upq, store_upv,
):
    reps = lax.axis_size("rep")
    core = jnp.bitwise_and(lax.axis_index("rep"), 1)
    same_core = [[r for r in range(reps) if r % 2 == k] for k in range(2)]
    other_core = [(r, r ^ 1) for r in range(reps)]
    n = STEPS * MIG
    kv = kv_cache.reshape(REQ, KV, HD)
    x = hidden.reshape(TOK, D)
    kvb = kv_base.reshape(STEPS * 2 * REQ, HD)
    slots = migrating.T

    core = core[None].astype(jnp.int32)

    packed = call(
        pack_kernel, "pack", jax.ShapeDtypeStruct((32, PIECE, 128), BF), [VM] * 3, nbytes=900000
    )(store_down.reshape(128, D), store_upq.reshape(RANK, D), store_upv.reshape(RANK, HD))
    got = lax.all_to_all(packed, "rep", 0, 0, tiled=True)

    mine, ids, lead, *which = call(
        message_kernel,
        "message",
        [
            jax.ShapeDtypeStruct((n, MSG, 128), BF),
            jax.ShapeDtypeStruct((TOK, 128), jnp.int32),
            jax.ShapeDtypeStruct((MIG, MSG, 128), BF),
        ]
        + [jax.ShapeDtypeStruct((1,), jnp.int32)] * STEPS,
        [SM] * 4 + [HBM] + [VM] * 3,
        [pltpu.VMEM((32 * n, 128), F32), pltpu.SemaphoreType.DMA((n,))],
        nbytes=1700000,
        out_specs=[VM] * 3 + [SM] * STEPS,
    )(slots, cache_lengths, pair_mask, adapter_ids, kv, x, kvb, adapter_ids)
    exchange = [
        (lambda v, bit=bit: lax.ppermute(v, "rep", [(r, r ^ (1 << bit)) for r in range(reps)]))
        for bit in range(reps.bit_length() - 1)
    ]

    def migrate(s, came):
        sent = pl.pallas_call(
            functools.partial(resolve_kernel, s),
            name="resolve%d" % s,
            grid=(1,),
            out_shape=jax.ShapeDtypeStruct((MIG, MSG, 128), BF),
            in_specs=[SM, pl.BlockSpec((MIG, MSG, 128), lambda i: (s, 0, 0))] + [VM] * s,
            out_specs=pl.BlockSpec((MIG, MSG, 128), lambda i: (0, 0, 0)),
            cost_estimate=pl.CostEstimate(flops=0, bytes_accessed=300000, transcendentals=0),
        )(slots, mine, *came)
        return lax.switch(which[s][0], exchange, sent)

    arr0 = lax.switch(which[0][0], exchange, lead)
    arr1 = migrate(1, [arr0])
    arr2 = migrate(2, [arr0, arr1])
    got, arr0, arr1, arr2 = lax.optimization_barrier((got, arr0, arr1, arr2))
    copies = call(
        pick_kernel, "pick", jax.ShapeDtypeStruct((16, 50 * STEPS, 128), BF), [SM, VM], nbytes=1400000, mib=8
    )(owners, got)
    own = lax.all_to_all(copies, "rep", 0, 0, tiled=True, axis_index_groups=same_core)
    arr3 = migrate(3, [arr0, arr1, arr2])
    own, arr3 = lax.optimization_barrier((own, arr3))
    oth = lax.ppermute(own, "rep", other_core)

    acc, tokens, all_ids = call(
        own_kernel,
        "project_own",
        [
            jax.ShapeDtypeStruct((ROWS, 128), F32),
            jax.ShapeDtypeStruct((ROWS, D), BF),
            jax.ShapeDtypeStruct((ROWS, 128), jnp.int32),
        ],
        [SM, HBM] + [VM] * 3 + [HBM, HBM, VM],
        [
            pltpu.VMEM((STEPS * 128, D // 2), BF),
            pltpu.VMEM((GHOST, D), F32),
            pltpu.VMEM((POOL * 128, D), BF),
            pltpu.SemaphoreType.DMA((3,)),
        ],
        flops=ROWS * D * SLOTS * 128,
        nbytes=4000000,
        out_specs=[VM] * 3,
        mib=12,
    )(core, x, arr1, arr2, arr3, ids, pool_down.reshape(POOL * 128, D), own)
    parts = call(
        other_kernel,
        "project_other",
        jax.ShapeDtypeStruct((8, ROWS, 128), BF),
        [SM] + [VM] * 4,
        [pltpu.VMEM((STEPS * 128, D // 2), BF)],
        flops=ROWS * D * SLOTS * 128,
        nbytes=2000000,
        mib=8,
    )(core, acc, tokens, all_ids, oth)
    parts, own, oth = lax.optimization_barrier((parts, own, oth))
    parts = lax.all_to_all(parts, "tp", 0, 0, tiled=True)
    wq, wv = call(
        prepare_kernel,
        "prepare",
        [jax.ShapeDtypeStruct((SLOTS * 128, D), BF), jax.ShapeDtypeStruct((SLOTS * 128, HD), BF)],
        [SM] + [VM] * 4,
        [pltpu.VMEM((STEPS * RANK, HD), F32)],
        nbytes=4000000,
        out_specs=[VM] * 2,
    )(core, pool_upq.reshape(POOL * RANK, D), pool_upv.reshape(POOL * RANK, HD), own, oth)
    parts, wq, wv = lax.optimization_barrier((parts, wq, wv))

    out = call(
        attend_kernel,
        "attend",
        jax.ShapeDtypeStruct((TOK, D), BF),
        [SM] * 2 + [VM] * 6 + [HBM] + [VM] * 4,
        [
            pltpu.VMEM((REQ + n, KV, HD), BF),
            pltpu.VMEM((REQ + n, 32, KV), BF),
            pltpu.VMEM((REQ * 32, HD), F32),
            pltpu.VMEM((REQ * 32, HD), F32),
            pltpu.VMEM((REQ * 8, HD), F32),
            pltpu.VMEM((STEPS * 2 * REQ, HD), F32),
            pltpu.VMEM((ROWS, HD), F32),
            pltpu.VMEM((32, HD), F32),
            pltpu.SemaphoreType.DMA((8,)),
        ],
        flops=2 * 72 * 32 * 256 * 128 * 2,
        nbytes=9000000,
    )(
        cache_lengths, slots, parts, all_ids, wq, wv, query_base.reshape(TOK, D), kvb, kv,
        arr0, arr1, arr2, arr3,
    )
    return out.reshape(STEPS, REQ, D)


def solution(mesh):
    return jax.shard_map(
        local,
        mesh=mesh,
        in_specs=(
            P(None, "rep", "tp"),
            P(None, "rep", "tp"),
            P(None, "rep", None, "tp"),
            P("rep", None, None, "tp"),
            P("rep"),
            P(None, "rep"),
            P(None, "rep"),
            P(),
            P(),
            P(None, None, None, "tp"),
            P(None, None, "tp"),
            P(None, None, "tp"),
            P("rep", None, None, "tp"),
            P("rep", None, "tp"),
            P("rep", None, "tp"),
        ),
        out_specs=P(None, "rep", "tp"),
        check_vma=False,
    )
```

```python
import functools
import math

import jax
import jax.numpy as jnp
from jax import lax
from jax.experimental import pallas as pl
from jax.experimental.pallas import tpu as pltpu
from jax.sharding import PartitionSpec as P

STEPS = 4
MIG = 2
POOL = 2
SLOTS = POOL + STEPS
REQ = 64
CTX = 128
HD = 128
HEADS = 8
D = 1024
RANK = 64
TOK = STEPS * REQ
GHOST = 16
ROWS = TOK + GHOST
MSG = 288
KV = 2 * CTX
PIECE = 56
F32 = jnp.float32
BF = jnp.bfloat16
NT = (((1,), (1,)), ((), ()))


VM = pl.BlockSpec(memory_space=pltpu.VMEM)
SM = pl.BlockSpec(memory_space=pltpu.SMEM)
HBM = pl.BlockSpec(memory_space=pltpu.HBM)

GHOSTS = [(s, j, t) for s in range(1, STEPS) for j in range(MIG) for t in range(s)]


def call(kernel, name, out_shape, in_specs, scratch=(), flops=0, nbytes=0, out_specs=VM, mib=None):
    return pl.pallas_call(
        kernel,
        name=name,
        out_shape=out_shape,
        in_specs=in_specs,
        out_specs=out_specs,
        scratch_shapes=list(scratch),
        cost_estimate=pl.CostEstimate(flops=flops, bytes_accessed=nbytes, transcendentals=0),
        compiler_params=pltpu.CompilerParams(vmem_limit_bytes=mib and mib << 20),
    )


def pack_kernel(down, upq, upv, out):
    values = upv[...].astype(F32)
    blank = jnp.zeros((6, HD), F32)
    for k in range(2):
        for p in range(16):
            g, b = p // 4, p % 4
            j = (p // 8) * 16 + (p % 8) * 2 + k
            cols = slice(512 * k + 128 * b, 512 * k + 128 * b + 128)
            out[j, 0:32, :] = down[32 * g : 32 * g + 32, cols]
            out[j, 32:48, :] = upq[16 * g : 16 * g + 16, cols]
            c = 2 * (16 * k + p)
            out[j, 48:56, :] = jnp.concatenate([values[c : c + 2], blank], axis=0).astype(BF)


def pick_kernel(owners, got, out):
    values = []
    for s in range(STEPS):
        piece = got[owners[s]]
        values.append(piece[48:56].astype(F32)[0:2])
        for p in range(16):
            out[p, 48 * s : 48 * s + 48, :] = piece[0:48]
    values = jnp.concatenate(values, axis=0).astype(BF)
    for p in range(16):
        out[p, 192:200, :] = values


def message_kernel(slots, lens, masks, adapters, kv_hbm, hidden, kvb, adapters_v, out, ids, lead, *rest):
    which, (tail, sem) = rest[:STEPS], rest[STEPS:]
    n = STEPS * MIG
    slot_of = [slots[m % MIG, m // MIG] for m in range(n)]
    copies = [
        pltpu.make_async_copy(kv_hbm.at[slot_of[m]], out.at[m, pl.ds(0, KV)], sem.at[m]) for m in range(n)
    ]
    for copy in copies:
        copy.start()
    for s in range(STEPS):
        mask = masks[s]
        which[s][0] = sum((mask >= (2 << b)).astype(jnp.int32) for b in range(4))
    row = lax.broadcasted_iota(jnp.int32, (n, 128), 0)
    lane = lax.broadcasted_iota(jnp.int32, (n, 128), 1)
    slot = jnp.zeros((n, 128), jnp.int32)
    for m in range(n):
        slot = jnp.where(row == m, slot_of[m], slot)
    one = jnp.where(lane == slot, 1.0, 0.0).astype(BF)[:, :REQ]
    key = jnp.where(lane == 2 * slot, 1.0, 0.0).astype(BF)
    val = jnp.where(lane == 2 * slot + 1, 1.0, 0.0).astype(BF)
    tags = jnp.zeros((n, 128), jnp.int32)
    for m in range(n):
        tags = jnp.where((row == m) & (lane == 0), lens[slot_of[m]], tags)
        for t in range(STEPS - 1):
            tags = jnp.where((row == m) & (lane == 1 + t), adapters[t, slot_of[m]], tags)
    for t in range(STEPS - 1):
        picked = jnp.dot(one, hidden[REQ * t : REQ * t + REQ, :], preferred_element_type=F32)
        for b in range(8):
            tail[pl.ds(8 * t + b, n, stride=32), :] = picked[:, 128 * b : 128 * b + 128]
        base = kvb[128 * t : 128 * t + 128, :]
        tail[pl.ds(24 + 2 * t, n, stride=32), :] = jnp.dot(key, base, preferred_element_type=F32)
        tail[pl.ds(25 + 2 * t, n, stride=32), :] = jnp.dot(val, base, preferred_element_type=F32)
    tail[pl.ds(30, n, stride=32), :] = tags.astype(F32)
    tail[pl.ds(31, n, stride=32), :] = jnp.zeros((n, 128), F32)
    for m in range(n):
        out[m, KV:MSG, :] = tail[32 * m : 32 * m + 32, :].astype(BF)
    down_row = lax.broadcasted_iota(jnp.int32, (REQ, REQ), 0)
    across = lax.broadcasted_iota(jnp.int32, (REQ, REQ), 1)
    for t in range(STEPS):
        spread = jnp.where(down_row == across, adapters_v[t : t + 1, :].astype(F32), 0.0)
        column = jnp.sum(spread, axis=1, keepdims=True)
        ids[REQ * t : REQ * t + REQ, :] = jnp.broadcast_to(column, (REQ, 128)).astype(jnp.int32)
    for m in range(MIG):
        lead[m, KV:MSG, :] = tail[32 * m : 32 * m + 32, :].astype(BF)
    for copy in copies:
        copy.wait()
    for m in range(MIG):
        lead[m, 0:KV, :] = out[m, 0:KV, :]


def resolve_kernel(step, slots, mine, *refs):
    earlier, out = refs[:-1], refs[-1]
    row = lax.broadcasted_iota(jnp.int32, (32, 128), 0)
    lane = lax.broadcasted_iota(jnp.int32, (32, 128), 1)
    made = jnp.where(row < 24, row // 8, (row - 24) // 2)
    made = jnp.where(row == 30, lane - 1, made)
    out[...] = mine[...]
    for e in range(step):
        for i in range(MIG):
            for j in range(MIG):

                @pl.when(slots[j, step] == slots[i, e])
                def _(e=e, i=i, j=j):
                    out[j, 0:KV, :] = earlier[e][i, 0:KV, :]
                    old = out[j, KV:MSG, :].astype(F32)
                    came = earlier[e][i, KV:MSG, :].astype(F32)
                    out[j, KV:MSG, :] = jnp.where(made < e, came, old).astype(BF)


def own_kernel(core, hidden, arr1, arr2, arr3, ids, pool_hbm, own, acc, x, all_ids, w, gx, pool, sem):
    copies = [
        pltpu.make_async_copy(hidden, x.at[pl.ds(0, TOK)], sem.at[0]),
        pltpu.make_async_copy(ids, all_ids.at[pl.ds(0, TOK)], sem.at[1]),
        pltpu.make_async_copy(pool_hbm, pool, sem.at[2]),
    ]
    for copy in copies:
        copy.start()
    mine = pl.multiple_of(core[0] * 512, 512)
    for s in range(STEPS):
        for p in range(16):
            g, b = p // 4, p % 4
            w[128 * s + 32 * g : 128 * s + 32 * g + 32, 128 * b : 128 * b + 128] = own[p, 48 * s : 48 * s + 32, :]
    all_ids[TOK:ROWS, :] = jnp.zeros((GHOST, 128), jnp.int32)
    gx[...] = jnp.zeros_like(gx)
    arrived = (None, arr1, arr2, arr3)
    for g, (s, j, t) in enumerate(GHOSTS):
        history = arrived[s][j, -32:, :].astype(F32)
        for b in range(8):
            gx[g : g + 1, 128 * b : 128 * b + 128] = history[8 * t + b : 8 * t + b + 1, :]
        tag = jnp.broadcast_to(history[30:31, 1 + t : 2 + t], (1, 128))
        all_ids[TOK + g : TOK + g + 1, :] = tag.astype(jnp.int32)
    x[TOK:ROWS, :] = gx[...].astype(BF)
    for copy in copies:
        copy.wait()
    total = jnp.zeros((ROWS, 128), F32)
    for a in range(POOL):
        part = lax.dot_general(x[...], pool[128 * a : 128 * a + 128, :], NT, preferred_element_type=F32)
        total = jnp.where(all_ids[...] == a, part, total)
    for s in range(STEPS):
        part = lax.dot_general(
            x[:, pl.ds(mine, 512)], w[128 * s : 128 * s + 128, :], NT, preferred_element_type=F32
        )
        total = jnp.where(all_ids[...] == POOL + s, part, total)
    acc[...] = total


def other_kernel(core, acc, x, all_ids, oth, out, w):
    theirs = pl.multiple_of(512 - core[0] * 512, 512)
    for s in range(STEPS):
        for p in range(16):
            g, b = p // 4, p % 4
            w[128 * s + 32 * g : 128 * s + 32 * g + 32, 128 * b : 128 * b + 128] = oth[p, 48 * s : 48 * s + 32, :]
    more = jnp.zeros((ROWS, 128), F32)
    for s in range(STEPS):
        part = lax.dot_general(
            x[:, pl.ds(theirs, 512)], w[128 * s : 128 * s + 128, :], NT, preferred_element_type=F32
        )
        more = jnp.where(all_ids[...] == POOL + s, part, more)
    total = (acc[...] + more).astype(BF)
    for c in range(8):
        out[c] = total


def prepare_kernel(core, pool_q, pool_v, own, oth, wq, wv, values):
    mine = core[0] * 512
    theirs = 512 - mine
    for a in range(SLOTS):
        wq[128 * a + RANK : 128 * a + 128, :] = jnp.zeros((RANK, D), BF)
        wv[128 * a : 128 * a + RANK, :] = jnp.zeros((RANK, HD), BF)
    for a in range(POOL):
        wq[128 * a : 128 * a + RANK, :] = pool_q[RANK * a : RANK * a + RANK, :]
        wv[128 * a + RANK : 128 * a + 128, :] = pool_v[RANK * a : RANK * a + RANK, :]
    for s in range(STEPS):
        top = 128 * (POOL + s)
        for p in range(16):
            g, b = p // 4, p % 4
            rows = slice(top + 16 * g, top + 16 * g + 16)
            wq[rows, pl.ds(pl.multiple_of(mine + 128 * b, 128), 128)] = own[p, 48 * s + 32 : 48 * s + 48, :]
            wq[rows, pl.ds(pl.multiple_of(theirs + 128 * b, 128), 128)] = oth[p, 48 * s + 32 : 48 * s + 48, :]
    half = 32 * core[0]
    for p in range(16):
        near = own[p, 192:200, :].astype(F32)
        far = oth[p, 192:200, :].astype(F32)
        for s in range(STEPS):
            values[pl.ds(RANK * s + half + 2 * p, 2), :] = near[2 * s : 2 * s + 2]
            values[pl.ds(RANK * s + 32 - half + 2 * p, 2), :] = far[2 * s : 2 * s + 2]
    for s in range(STEPS):
        top = 128 * (POOL + s) + RANK
        wv[top : top + RANK, :] = values[RANK * s : RANK * s + RANK, :].astype(BF)


def attend_kernel(
    lens, slots, parts, ids, wq, wv, qb, kvb, kv_hbm, arr0, arr1, arr2, arr3,
    out, kv, ws, qs, os, ts, base, dv, tails, sem,
):
    copies = [
        pltpu.make_async_copy(kv_hbm.at[pl.ds(8 * b, 8)], kv.at[pl.ds(8 * b, 8)], sem.at[b])
        for b in range(8)
    ]
    for copy in copies:
        copy.start()
    arrived = (arr0, arr1, arr2, arr3)

    u = parts[0].astype(F32)
    for c in range(1, 8):
        u = u + parts[c].astype(F32)
    spread = jnp.concatenate([jnp.where(ids[...] == a, u, 0.0).astype(BF) for a in range(SLOTS)], axis=1)
    dv[...] = jnp.dot(spread, wv[...], preferred_element_type=F32)
    dq = jnp.dot(spread[:TOK], wq[...], preferred_element_type=F32)
    base[...] = kvb[...].astype(F32)
    for t in range(STEPS):
        for h in range(HEADS):
            cols = slice(HD * h, HD * h + HD)
            query = qb[REQ * t : REQ * t + REQ, cols].astype(F32) + dq[REQ * t : REQ * t + REQ, cols]
            qs[pl.ds(8 * t + h, REQ, stride=32), :] = query
        ts[pl.ds(2 * t, REQ, stride=8), :] = base[pl.ds(128 * t, REQ, stride=2), :]
        ts[pl.ds(2 * t + 1, REQ, stride=8), :] = (
            base[pl.ds(128 * t + 1, REQ, stride=2), :] + dv[REQ * t : REQ * t + REQ, :]
        )

    col = lax.broadcasted_iota(jnp.int32, (32, KV), 1)
    step_of = lax.broadcasted_iota(jnp.int32, (32, KV), 0) // HEADS
    reach = jnp.where(col % 2 == 0, col - 2 * step_of, 4 * KV)
    row32 = lax.broadcasted_iota(jnp.int32, (32, HD), 0)
    row8 = lax.broadcasted_iota(jnp.int32, (8, HD), 0)

    def weigh(i, slot, length, tok):
        first = 2 * length
        start = pl.multiple_of(jnp.minimum((first // 16) * 16, KV - 32), 16)
        off = first - start
        turned = pltpu.roll(tok, off % 8, 0)
        turned = jnp.concatenate([turned] * 4, axis=0)
        window = kv[i, pl.ds(start, 32), :].astype(F32)
        inside = (row32 >= off) & (row32 < off + 8)
        kv[i, pl.ds(start, 32), :] = jnp.where(inside, turned, window).astype(BF)
        q = qs[pl.ds(pl.multiple_of(32 * slot, 32), 32), :].astype(BF)
        score = lax.dot_general(q, kv[i], NT, preferred_element_type=F32) * (1.0 / math.sqrt(HD))
        score = jnp.where(reach <= first, score, -1e30)
        e = jnp.exp(score - jnp.max(score, axis=1, keepdims=True))
        weight = e * (1.0 / jnp.sum(e, axis=1, keepdims=True))
        ws[i] = pltpu.roll(weight, 1, 1).astype(BF)

    def weigh_block(b, carry):
        for c in range(2):
            eight = pl.ds(16 * b + 8 * c, 8)
            pltpu.make_async_copy(kv_hbm.at[eight], kv.at[eight], sem.at[2 * b + c]).wait()
        for r in range(16):
            i = 16 * b + r
            weigh(i, i, lens[i], ts[pl.ds(pl.multiple_of(8 * i, 8), 8), :])
        return carry

    def mix_block(b, carry):
        for r in range(32):
            i = 32 * b + r
            mixed = jnp.dot(ws[i], kv[i], preferred_element_type=F32)
            os[pl.ds(pl.multiple_of(32 * i, 32), 32), :] = mixed
        return carry

    lax.fori_loop(0, 4, weigh_block, 0)
    for s in range(STEPS):
        for j in range(MIG):
            a = MIG * s + j
            kv[REQ + a] = arrived[s][j, 0:KV, :]
            tails[...] = arrived[s][j, KV:MSG, :].astype(F32)
            slot = slots[j, s]
            tok = ts[pl.ds(pl.multiple_of(8 * slot, 8), 8), :]
            for t in range(s):
                g = TOK + GHOSTS.index((s, j, t))
                tok = jnp.where(row8 == 2 * t, tails[24 + 2 * t : 25 + 2 * t, :], tok)
                new = tails[25 + 2 * t : 26 + 2 * t, :] + dv[g : g + 1, :]
                tok = jnp.where(row8 == 2 * t + 1, new, tok)
            length = jnp.max(tails[30:31, 0:1]).astype(jnp.int32)
            weigh(REQ + a, slot, length, tok)
    lax.fori_loop(0, 2, mix_block, 0)
    for s in range(STEPS):
        for j in range(MIG):
            a = MIG * s + j
            keep = HEADS * s
            mixed = jnp.dot(ws[REQ + a], kv[REQ + a], preferred_element_type=F32)
            rows = pl.ds(pl.multiple_of(32 * slots[j, s] + keep, 8), 32 - keep)
            os[rows, :] = mixed[keep:, :]

    for t in range(STEPS):
        for h in range(HEADS):
            out[REQ * t : REQ * t + REQ, HD * h : HD * h + HD] = os[
                pl.ds(8 * t + h, REQ, stride=32), :
            ].astype(BF)


def local(
    hidden, query_base, kv_base, kv_cache, cache_lengths, adapter_ids, migrating, pair_mask,
    owners, pool_down, pool_upq, pool_upv, store_down, store_upq, store_upv,
):
    reps = lax.axis_size("rep")
    core = jnp.bitwise_and(lax.axis_index("rep"), 1)
    same_core = [[r for r in range(reps) if r % 2 == k] for k in range(2)]
    other_core = [(r, r ^ 1) for r in range(reps)]
    n = STEPS * MIG
    kv = kv_cache.reshape(REQ, KV, HD)
    x = hidden.reshape(TOK, D)
    kvb = kv_base.reshape(STEPS * 2 * REQ, HD)
    slots = migrating.T

    core = core[None].astype(jnp.int32)

    packed = call(
        pack_kernel, "pack", jax.ShapeDtypeStruct((32, PIECE, 128), BF), [VM] * 3, nbytes=900000
    )(store_down.reshape(128, D), store_upq.reshape(RANK, D), store_upv.reshape(RANK, HD))
    got = lax.all_to_all(packed, "rep", 0, 0, tiled=True)

    mine, ids, lead, *which = call(
        message_kernel,
        "message",
        [
            jax.ShapeDtypeStruct((n, MSG, 128), BF),
            jax.ShapeDtypeStruct((TOK, 128), jnp.int32),
            jax.ShapeDtypeStruct((MIG, MSG, 128), BF),
        ]
        + [jax.ShapeDtypeStruct((1,), jnp.int32)] * STEPS,
        [SM] * 4 + [HBM] + [VM] * 3,
        [pltpu.VMEM((32 * n, 128), F32), pltpu.SemaphoreType.DMA((n,))],
        nbytes=1700000,
        out_specs=[VM] * 3 + [SM] * STEPS,
    )(slots, cache_lengths, pair_mask, adapter_ids, kv, x, kvb, adapter_ids)
    exchange = [
        (lambda v, bit=bit: lax.ppermute(v, "rep", [(r, r ^ (1 << bit)) for r in range(reps)]))
        for bit in range(reps.bit_length() - 1)
    ]

    def migrate(s, came):
        sent = pl.pallas_call(
            functools.partial(resolve_kernel, s),
            name="resolve%d" % s,
            grid=(1,),
            out_shape=jax.ShapeDtypeStruct((MIG, MSG, 128), BF),
            in_specs=[SM, pl.BlockSpec((MIG, MSG, 128), lambda i: (s, 0, 0))] + [VM] * s,
            out_specs=pl.BlockSpec((MIG, MSG, 128), lambda i: (0, 0, 0)),
            cost_estimate=pl.CostEstimate(flops=0, bytes_accessed=300000, transcendentals=0),
        )(slots, mine, *came)
        return lax.switch(which[s][0], exchange, sent)

    arr0 = lax.switch(which[0][0], exchange, lead)
    arr1 = migrate(1, [arr0])
    got, arr0, arr1 = lax.optimization_barrier((got, arr0, arr1))
    copies = call(
        pick_kernel, "pick", jax.ShapeDtypeStruct((16, 50 * STEPS, 128), BF), [SM, VM], nbytes=1400000, mib=8
    )(owners, got)
    own = lax.all_to_all(copies, "rep", 0, 0, tiled=True, axis_index_groups=same_core)
    arr2 = migrate(2, [arr0, arr1])
    arr3 = migrate(3, [arr0, arr1, arr2])
    own, arr2, arr3 = lax.optimization_barrier((own, arr2, arr3))
    oth = lax.ppermute(own, "rep", other_core)

    acc, tokens, all_ids = call(
        own_kernel,
        "project_own",
        [
            jax.ShapeDtypeStruct((ROWS, 128), F32),
            jax.ShapeDtypeStruct((ROWS, D), BF),
            jax.ShapeDtypeStruct((ROWS, 128), jnp.int32),
        ],
        [SM, HBM] + [VM] * 3 + [HBM, HBM, VM],
        [
            pltpu.VMEM((STEPS * 128, D // 2), BF),
            pltpu.VMEM((GHOST, D), F32),
            pltpu.VMEM((POOL * 128, D), BF),
            pltpu.SemaphoreType.DMA((3,)),
        ],
        flops=ROWS * D * SLOTS * 128,
        nbytes=4000000,
        out_specs=[VM] * 3,
        mib=12,
    )(core, x, arr1, arr2, arr3, ids, pool_down.reshape(POOL * 128, D), own)
    parts = call(
        other_kernel,
        "project_other",
        jax.ShapeDtypeStruct((8, ROWS, 128), BF),
        [SM] + [VM] * 4,
        [pltpu.VMEM((STEPS * 128, D // 2), BF)],
        flops=ROWS * D * SLOTS * 128,
        nbytes=2000000,
        mib=8,
    )(core, acc, tokens, all_ids, oth)
    parts, own, oth = lax.optimization_barrier((parts, own, oth))
    parts = lax.all_to_all(parts, "tp", 0, 0, tiled=True)
    wq, wv = call(
        prepare_kernel,
        "prepare",
        [jax.ShapeDtypeStruct((SLOTS * 128, D), BF), jax.ShapeDtypeStruct((SLOTS * 128, HD), BF)],
        [SM] + [VM] * 4,
        [pltpu.VMEM((STEPS * RANK, HD), F32)],
        nbytes=4000000,
        out_specs=[VM] * 2,
    )(core, pool_upq.reshape(POOL * RANK, D), pool_upv.reshape(POOL * RANK, HD), own, oth)
    parts, wq, wv = lax.optimization_barrier((parts, wq, wv))

    out = call(
        attend_kernel,
        "attend",
        jax.ShapeDtypeStruct((TOK, D), BF),
        [SM] * 2 + [VM] * 6 + [HBM] + [VM] * 4,
        [
            pltpu.VMEM((REQ + n, KV, HD), BF),
            pltpu.VMEM((REQ + n, 32, KV), BF),
            pltpu.VMEM((REQ * 32, HD), F32),
            pltpu.VMEM((REQ * 32, HD), F32),
            pltpu.VMEM((REQ * 8, HD), F32),
            pltpu.VMEM((STEPS * 2 * REQ, HD), F32),
            pltpu.VMEM((ROWS, HD), F32),
            pltpu.VMEM((32, HD), F32),
            pltpu.SemaphoreType.DMA((8,)),
        ],
        flops=2 * 72 * 32 * 256 * 128 * 2,
        nbytes=9000000,
    )(
        cache_lengths, slots, parts, all_ids, wq, wv, query_base.reshape(TOK, D), kvb, kv,
        arr0, arr1, arr2, arr3,
    )
    return out.reshape(STEPS, REQ, D)


def solution(mesh):
    return jax.shard_map(
        local,
        mesh=mesh,
        in_specs=(
            P(None, "rep", "tp"),
            P(None, "rep", "tp"),
            P(None, "rep", None, "tp"),
            P("rep", None, None, "tp"),
            P("rep"),
            P(None, "rep"),
            P(None, "rep"),
            P(),
            P(),
            P(None, None, None, "tp"),
            P(None, None, "tp"),
            P(None, None, "tp"),
            P("rep", None, None, "tp"),
            P("rep", None, "tp"),
            P("rep", None, "tp"),
        ),
        out_specs=P(None, "rep", "tp"),
        check_vma=False,
    )
```

```python
import functools
import math

import jax
import jax.numpy as jnp
from jax import lax
from jax.experimental import pallas as pl
from jax.experimental.pallas import tpu as pltpu
from jax.sharding import PartitionSpec as P

STEPS = 4
MIG = 2
POOL = 2
SLOTS = POOL + STEPS
REQ = 64
CTX = 128
HD = 128
HEADS = 8
D = 1024
RANK = 64
TOK = STEPS * REQ
GHOST = 16
ROWS = TOK + GHOST
MSG = 288
KV = 2 * CTX
PIECE = 56
F32 = jnp.float32
BF = jnp.bfloat16
NT = (((1,), (1,)), ((), ()))


VM = pl.BlockSpec(memory_space=pltpu.VMEM)
SM = pl.BlockSpec(memory_space=pltpu.SMEM)
HBM = pl.BlockSpec(memory_space=pltpu.HBM)

GHOSTS = [(s, j, t) for s in range(1, STEPS) for j in range(MIG) for t in range(s)]


def call(kernel, name, out_shape, in_specs, scratch=(), flops=0, nbytes=0, out_specs=VM, mib=None):
    return pl.pallas_call(
        kernel,
        name=name,
        out_shape=out_shape,
        in_specs=in_specs,
        out_specs=out_specs,
        scratch_shapes=list(scratch),
        cost_estimate=pl.CostEstimate(flops=flops, bytes_accessed=nbytes, transcendentals=0),
        compiler_params=pltpu.CompilerParams(vmem_limit_bytes=mib and mib << 20),
    )


def pack_kernel(down, upq, upv, out):
    values = upv[...].astype(F32)
    blank = jnp.zeros((6, HD), F32)
    for k in range(2):
        for p in range(16):
            g, b = p // 4, p % 4
            j = (p // 8) * 16 + (p % 8) * 2 + k
            cols = slice(512 * k + 128 * b, 512 * k + 128 * b + 128)
            out[j, 0:32, :] = down[32 * g : 32 * g + 32, cols]
            out[j, 32:48, :] = upq[16 * g : 16 * g + 16, cols]
            c = 2 * (16 * k + p)
            out[j, 48:56, :] = jnp.concatenate([values[c : c + 2], blank], axis=0).astype(BF)


def pick_kernel(owners, got, out):
    values = []
    for s in range(STEPS):
        piece = got[owners[s]]
        values.append(piece[48:56].astype(F32)[0:2])
        for p in range(16):
            out[p, 48 * s : 48 * s + 48, :] = piece[0:48]
    values = jnp.concatenate(values, axis=0).astype(BF)
    for p in range(16):
        out[p, 192:200, :] = values


def message_kernel(slots, lens, masks, adapters, kv_hbm, hidden, kvb, adapters_v, out, ids, lead, *rest):
    which, (tail, sem) = rest[:STEPS], rest[STEPS:]
    n = STEPS * MIG
    slot_of = [slots[m % MIG, m // MIG] for m in range(n)]
    copies = [
        pltpu.make_async_copy(kv_hbm.at[slot_of[m]], out.at[m, pl.ds(0, KV)], sem.at[m]) for m in range(n)
    ]
    for copy in copies:
        copy.start()
    for s in range(STEPS):
        mask = masks[s]
        which[s][0] = sum((mask >= (2 << b)).astype(jnp.int32) for b in range(4))
    row = lax.broadcasted_iota(jnp.int32, (n, 128), 0)
    lane = lax.broadcasted_iota(jnp.int32, (n, 128), 1)
    slot = jnp.zeros((n, 128), jnp.int32)
    for m in range(n):
        slot = jnp.where(row == m, slot_of[m], slot)
    one = jnp.where(lane == slot, 1.0, 0.0).astype(BF)[:, :REQ]
    key = jnp.where(lane == 2 * slot, 1.0, 0.0).astype(BF)
    val = jnp.where(lane == 2 * slot + 1, 1.0, 0.0).astype(BF)
    tags = jnp.zeros((n, 128), jnp.int32)
    for m in range(n):
        tags = jnp.where((row == m) & (lane == 0), lens[slot_of[m]], tags)
        for t in range(STEPS - 1):
            tags = jnp.where((row == m) & (lane == 1 + t), adapters[t, slot_of[m]], tags)
    for t in range(STEPS - 1):
        picked = jnp.dot(one, hidden[REQ * t : REQ * t + REQ, :], preferred_element_type=F32)
        for b in range(8):
            tail[pl.ds(8 * t + b, n, stride=32), :] = picked[:, 128 * b : 128 * b + 128]
        base = kvb[128 * t : 128 * t + 128, :]
        tail[pl.ds(24 + 2 * t, n, stride=32), :] = jnp.dot(key, base, preferred_element_type=F32)
        tail[pl.ds(25 + 2 * t, n, stride=32), :] = jnp.dot(val, base, preferred_element_type=F32)
    tail[pl.ds(30, n, stride=32), :] = tags.astype(F32)
    tail[pl.ds(31, n, stride=32), :] = jnp.zeros((n, 128), F32)
    for m in range(n):
        out[m, KV:MSG, :] = tail[32 * m : 32 * m + 32, :].astype(BF)
    down_row = lax.broadcasted_iota(jnp.int32, (REQ, REQ), 0)
    across = lax.broadcasted_iota(jnp.int32, (REQ, REQ), 1)
    for t in range(STEPS):
        spread = jnp.where(down_row == across, adapters_v[t : t + 1, :].astype(F32), 0.0)
        column = jnp.sum(spread, axis=1, keepdims=True)
        ids[REQ * t : REQ * t + REQ, :] = jnp.broadcast_to(column, (REQ, 128)).astype(jnp.int32)
    for m in range(MIG):
        lead[m, KV:MSG, :] = tail[32 * m : 32 * m + 32, :].astype(BF)
    for copy in copies:
        copy.wait()
    for m in range(MIG):
        lead[m, 0:KV, :] = out[m, 0:KV, :]


def resolve_kernel(step, slots, mine, *refs):
    earlier, out = refs[:-1], refs[-1]
    row = lax.broadcasted_iota(jnp.int32, (32, 128), 0)
    lane = lax.broadcasted_iota(jnp.int32, (32, 128), 1)
    made = jnp.where(row < 24, row // 8, (row - 24) // 2)
    made = jnp.where(row == 30, lane - 1, made)
    out[...] = mine[...]
    for e in range(step):
        for i in range(MIG):
            for j in range(MIG):

                @pl.when(slots[j, step] == slots[i, e])
                def _(e=e, i=i, j=j):
                    out[j, 0:KV, :] = earlier[e][i, 0:KV, :]
                    old = out[j, KV:MSG, :].astype(F32)
                    came = earlier[e][i, KV:MSG, :].astype(F32)
                    out[j, KV:MSG, :] = jnp.where(made < e, came, old).astype(BF)


def own_kernel(core, hidden, arr1, arr2, arr3, ids, pool_hbm, own, acc, x, all_ids, w, gx, pool, sem):
    copies = [
        pltpu.make_async_copy(hidden, x.at[pl.ds(0, TOK)], sem.at[0]),
        pltpu.make_async_copy(ids, all_ids.at[pl.ds(0, TOK)], sem.at[1]),
        pltpu.make_async_copy(pool_hbm, pool, sem.at[2]),
    ]
    for copy in copies:
        copy.start()
    mine = pl.multiple_of(core[0] * 512, 512)
    for s in range(STEPS):
        for p in range(16):
            g, b = p // 4, p % 4
            w[128 * s + 32 * g : 128 * s + 32 * g + 32, 128 * b : 128 * b + 128] = own[p, 48 * s : 48 * s + 32, :]
    all_ids[TOK:ROWS, :] = jnp.zeros((GHOST, 128), jnp.int32)
    gx[...] = jnp.zeros_like(gx)
    arrived = (None, arr1, arr2, arr3)
    for g, (s, j, t) in enumerate(GHOSTS):
        history = arrived[s][j, -32:, :].astype(F32)
        for b in range(8):
            gx[g : g + 1, 128 * b : 128 * b + 128] = history[8 * t + b : 8 * t + b + 1, :]
        tag = jnp.broadcast_to(history[30:31, 1 + t : 2 + t], (1, 128))
        all_ids[TOK + g : TOK + g + 1, :] = tag.astype(jnp.int32)
    x[TOK:ROWS, :] = gx[...].astype(BF)
    for copy in copies:
        copy.wait()
    total = jnp.zeros((ROWS, 128), F32)
    for a in range(POOL):
        part = lax.dot_general(x[...], pool[128 * a : 128 * a + 128, :], NT, preferred_element_type=F32)
        total = jnp.where(all_ids[...] == a, part, total)
    for s in range(STEPS):
        part = lax.dot_general(
            x[:, pl.ds(mine, 512)], w[128 * s : 128 * s + 128, :], NT, preferred_element_type=F32
        )
        total = jnp.where(all_ids[...] == POOL + s, part, total)
    acc[...] = total


def other_kernel(core, acc, x, all_ids, oth, out, w):
    theirs = pl.multiple_of(512 - core[0] * 512, 512)
    for s in range(STEPS):
        for p in range(16):
            g, b = p // 4, p % 4
            w[128 * s + 32 * g : 128 * s + 32 * g + 32, 128 * b : 128 * b + 128] = oth[p, 48 * s : 48 * s + 32, :]
    more = jnp.zeros((ROWS, 128), F32)
    for s in range(STEPS):
        part = lax.dot_general(
            x[:, pl.ds(theirs, 512)], w[128 * s : 128 * s + 128, :], NT, preferred_element_type=F32
        )
        more = jnp.where(all_ids[...] == POOL + s, part, more)
    total = (acc[...] + more).astype(BF)
    for c in range(8):
        out[c] = total


def prepare_kernel(core, pool_q, pool_v, own, oth, wq, wv, values):
    mine = core[0] * 512
    theirs = 512 - mine
    for a in range(SLOTS):
        wq[128 * a + RANK : 128 * a + 128, :] = jnp.zeros((RANK, D), BF)
        wv[128 * a : 128 * a + RANK, :] = jnp.zeros((RANK, HD), BF)
    for a in range(POOL):
        wq[128 * a : 128 * a + RANK, :] = pool_q[RANK * a : RANK * a + RANK, :]
        wv[128 * a + RANK : 128 * a + 128, :] = pool_v[RANK * a : RANK * a + RANK, :]
    for s in range(STEPS):
        top = 128 * (POOL + s)
        for p in range(16):
            g, b = p // 4, p % 4
            rows = slice(top + 16 * g, top + 16 * g + 16)
            wq[rows, pl.ds(pl.multiple_of(mine + 128 * b, 128), 128)] = own[p, 48 * s + 32 : 48 * s + 48, :]
            wq[rows, pl.ds(pl.multiple_of(theirs + 128 * b, 128), 128)] = oth[p, 48 * s + 32 : 48 * s + 48, :]
    half = 32 * core[0]
    for p in range(16):
        near = own[p, 192:200, :].astype(F32)
        far = oth[p, 192:200, :].astype(F32)
        for s in range(STEPS):
            values[pl.ds(RANK * s + half + 2 * p, 2), :] = near[2 * s : 2 * s + 2]
            values[pl.ds(RANK * s + 32 - half + 2 * p, 2), :] = far[2 * s : 2 * s + 2]
    for s in range(STEPS):
        top = 128 * (POOL + s) + RANK
        wv[top : top + RANK, :] = values[RANK * s : RANK * s + RANK, :].astype(BF)


def attend_kernel(
    lens, slots, parts, ids, wq, wv, qb, kvb, kv_hbm, arr0, arr1, arr2, arr3,
    out, kv, ws, qs, os, ts, base, dv, tails, sem,
):
    copies = [
        pltpu.make_async_copy(kv_hbm.at[pl.ds(8 * b, 8)], kv.at[pl.ds(8 * b, 8)], sem.at[b])
        for b in range(8)
    ]
    for copy in copies:
        copy.start()
    arrived = (arr0, arr1, arr2, arr3)

    u = parts[0].astype(F32)
    for c in range(1, 8):
        u = u + parts[c].astype(F32)
    spread = jnp.concatenate([jnp.where(ids[...] == a, u, 0.0).astype(BF) for a in range(SLOTS)], axis=1)
    dv[...] = jnp.dot(spread, wv[...], preferred_element_type=F32)
    dq = jnp.dot(spread[:TOK], wq[...], preferred_element_type=F32)
    base[...] = kvb[...].astype(F32)
    for t in range(STEPS):
        for h in range(HEADS):
            cols = slice(HD * h, HD * h + HD)
            query = qb[REQ * t : REQ * t + REQ, cols].astype(F32) + dq[REQ * t : REQ * t + REQ, cols]
            qs[pl.ds(8 * t + h, REQ, stride=32), :] = query
        ts[pl.ds(2 * t, REQ, stride=8), :] = base[pl.ds(128 * t, REQ, stride=2), :]
        ts[pl.ds(2 * t + 1, REQ, stride=8), :] = (
            base[pl.ds(128 * t + 1, REQ, stride=2), :] + dv[REQ * t : REQ * t + REQ, :]
        )

    col = lax.broadcasted_iota(jnp.int32, (32, KV), 1)
    step_of = lax.broadcasted_iota(jnp.int32, (32, KV), 0) // HEADS
    reach = jnp.where(col % 2 == 0, col - 2 * step_of, 4 * KV)
    row32 = lax.broadcasted_iota(jnp.int32, (32, HD), 0)
    row8 = lax.broadcasted_iota(jnp.int32, (8, HD), 0)

    def weigh(i, slot, length, tok):
        first = 2 * length
        start = pl.multiple_of(jnp.minimum((first // 16) * 16, KV - 32), 16)
        off = first - start
        turned = pltpu.roll(tok, off % 8, 0)
        turned = jnp.concatenate([turned] * 4, axis=0)
        window = kv[i, pl.ds(start, 32), :].astype(F32)
        inside = (row32 >= off) & (row32 < off + 8)
        kv[i, pl.ds(start, 32), :] = jnp.where(inside, turned, window).astype(BF)
        q = qs[pl.ds(pl.multiple_of(32 * slot, 32), 32), :].astype(BF)
        score = lax.dot_general(q, kv[i], NT, preferred_element_type=F32) * (1.0 / math.sqrt(HD))
        score = jnp.where(reach <= first, score, -1e30)
        e = jnp.exp(score - jnp.max(score, axis=1, keepdims=True))
        weight = e * (1.0 / jnp.sum(e, axis=1, keepdims=True))
        ws[i] = pltpu.roll(weight, 1, 1).astype(BF)

    def weigh_block(b, carry):
        for c in range(2):
            eight = pl.ds(16 * b + 8 * c, 8)
            pltpu.make_async_copy(kv_hbm.at[eight], kv.at[eight], sem.at[2 * b + c]).wait()
        for r in range(16):
            i = 16 * b + r
            weigh(i, i, lens[i], ts[pl.ds(pl.multiple_of(8 * i, 8), 8), :])
        return carry

    lax.fori_loop(0, 4, weigh_block, 0)
    for s in range(STEPS):
        for j in range(MIG):
            a = MIG * s + j
            kv[REQ + a] = arrived[s][j, 0:KV, :]
            tails[...] = arrived[s][j, KV:MSG, :].astype(F32)
            slot = slots[j, s]
            tok = ts[pl.ds(pl.multiple_of(8 * slot, 8), 8), :]
            for t in range(s):
                g = TOK + GHOSTS.index((s, j, t))
                tok = jnp.where(row8 == 2 * t, tails[24 + 2 * t : 25 + 2 * t, :], tok)
                new = tails[25 + 2 * t : 26 + 2 * t, :] + dv[g : g + 1, :]
                tok = jnp.where(row8 == 2 * t + 1, new, tok)
            length = jnp.max(tails[30:31, 0:1]).astype(jnp.int32)
            weigh(REQ + a, slot, length, tok)
    for i in range(REQ):
        os[32 * i : 32 * i + 32, :] = jnp.dot(ws[i], kv[i], preferred_element_type=F32)
    for s in range(STEPS):
        for j in range(MIG):
            a = MIG * s + j
            keep = HEADS * s
            mixed = jnp.dot(ws[REQ + a], kv[REQ + a], preferred_element_type=F32)
            rows = pl.ds(pl.multiple_of(32 * slots[j, s] + keep, 8), 32 - keep)
            os[rows, :] = mixed[keep:, :]

    for t in range(STEPS):
        for h in range(HEADS):
            out[REQ * t : REQ * t + REQ, HD * h : HD * h + HD] = os[
                pl.ds(8 * t + h, REQ, stride=32), :
            ].astype(BF)


def local(
    hidden, query_base, kv_base, kv_cache, cache_lengths, adapter_ids, migrating, pair_mask,
    owners, pool_down, pool_upq, pool_upv, store_down, store_upq, store_upv,
):
    reps = lax.axis_size("rep")
    core = jnp.bitwise_and(lax.axis_index("rep"), 1)
    same_core = [[r for r in range(reps) if r % 2 == k] for k in range(2)]
    other_core = [(r, r ^ 1) for r in range(reps)]
    n = STEPS * MIG
    kv = kv_cache.reshape(REQ, KV, HD)
    x = hidden.reshape(TOK, D)
    kvb = kv_base.reshape(STEPS * 2 * REQ, HD)
    slots = migrating.T

    core = core[None].astype(jnp.int32)

    packed = call(
        pack_kernel, "pack", jax.ShapeDtypeStruct((32, PIECE, 128), BF), [VM] * 3, nbytes=900000
    )(store_down.reshape(128, D), store_upq.reshape(RANK, D), store_upv.reshape(RANK, HD))
    got = lax.all_to_all(packed, "rep", 0, 0, tiled=True)

    mine, ids, lead, *which = call(
        message_kernel,
        "message",
        [
            jax.ShapeDtypeStruct((n, MSG, 128), BF),
            jax.ShapeDtypeStruct((TOK, 128), jnp.int32),
            jax.ShapeDtypeStruct((MIG, MSG, 128), BF),
        ]
        + [jax.ShapeDtypeStruct((1,), jnp.int32)] * STEPS,
        [SM] * 4 + [HBM] + [VM] * 3,
        [pltpu.VMEM((32 * n, 128), F32), pltpu.SemaphoreType.DMA((n,))],
        nbytes=1700000,
        out_specs=[VM] * 3 + [SM] * STEPS,
    )(slots, cache_lengths, pair_mask, adapter_ids, kv, x, kvb, adapter_ids)
    exchange = [
        (lambda v, bit=bit: lax.ppermute(v, "rep", [(r, r ^ (1 << bit)) for r in range(reps)]))
        for bit in range(reps.bit_length() - 1)
    ]

    def migrate(s, came):
        sent = pl.pallas_call(
            functools.partial(resolve_kernel, s),
            name="resolve%d" % s,
            grid=(1,),
            out_shape=jax.ShapeDtypeStruct((MIG, MSG, 128), BF),
            in_specs=[SM, pl.BlockSpec((MIG, MSG, 128), lambda i: (s, 0, 0))] + [VM] * s,
            out_specs=pl.BlockSpec((MIG, MSG, 128), lambda i: (0, 0, 0)),
            cost_estimate=pl.CostEstimate(flops=0, bytes_accessed=300000, transcendentals=0),
        )(slots, mine, *came)
        return lax.switch(which[s][0], exchange, sent)

    arr0 = lax.switch(which[0][0], exchange, lead)
    arr1 = migrate(1, [arr0])
    got, arr0, arr1 = lax.optimization_barrier((got, arr0, arr1))
    copies = call(
        pick_kernel, "pick", jax.ShapeDtypeStruct((16, 50 * STEPS, 128), BF), [SM, VM], nbytes=1400000, mib=8
    )(owners, got)
    own = lax.all_to_all(copies, "rep", 0, 0, tiled=True, axis_index_groups=same_core)
    arr2 = migrate(2, [arr0, arr1])
    arr3 = migrate(3, [arr0, arr1, arr2])
    own, arr2, arr3 = lax.optimization_barrier((own, arr2, arr3))
    oth = lax.ppermute(own, "rep", other_core)

    acc, tokens, all_ids = call(
        own_kernel,
        "project_own",
        [
            jax.ShapeDtypeStruct((ROWS, 128), F32),
            jax.ShapeDtypeStruct((ROWS, D), BF),
            jax.ShapeDtypeStruct((ROWS, 128), jnp.int32),
        ],
        [SM, HBM] + [VM] * 3 + [HBM, HBM, VM],
        [
            pltpu.VMEM((STEPS * 128, D // 2), BF),
            pltpu.VMEM((GHOST, D), F32),
            pltpu.VMEM((POOL * 128, D), BF),
            pltpu.SemaphoreType.DMA((3,)),
        ],
        flops=ROWS * D * SLOTS * 128,
        nbytes=4000000,
        out_specs=[VM] * 3,
        mib=12,
    )(core, x, arr1, arr2, arr3, ids, pool_down.reshape(POOL * 128, D), own)
    parts = call(
        other_kernel,
        "project_other",
        jax.ShapeDtypeStruct((8, ROWS, 128), BF),
        [SM] + [VM] * 4,
        [pltpu.VMEM((STEPS * 128, D // 2), BF)],
        flops=ROWS * D * SLOTS * 128,
        nbytes=2000000,
        mib=8,
    )(core, acc, tokens, all_ids, oth)
    parts, own, oth = lax.optimization_barrier((parts, own, oth))
    parts = lax.all_to_all(parts, "tp", 0, 0, tiled=True)
    wq, wv = call(
        prepare_kernel,
        "prepare",
        [jax.ShapeDtypeStruct((SLOTS * 128, D), BF), jax.ShapeDtypeStruct((SLOTS * 128, HD), BF)],
        [SM] + [VM] * 4,
        [pltpu.VMEM((STEPS * RANK, HD), F32)],
        nbytes=4000000,
        out_specs=[VM] * 2,
    )(core, pool_upq.reshape(POOL * RANK, D), pool_upv.reshape(POOL * RANK, HD), own, oth)
    parts, wq, wv = lax.optimization_barrier((parts, wq, wv))

    out = call(
        attend_kernel,
        "attend",
        jax.ShapeDtypeStruct((TOK, D), BF),
        [SM] * 2 + [VM] * 6 + [HBM] + [VM] * 4,
        [
            pltpu.VMEM((REQ + n, KV, HD), BF),
            pltpu.VMEM((REQ + n, 32, KV), BF),
            pltpu.VMEM((REQ * 32, HD), F32),
            pltpu.VMEM((REQ * 32, HD), F32),
            pltpu.VMEM((REQ * 8, HD), F32),
            pltpu.VMEM((STEPS * 2 * REQ, HD), F32),
            pltpu.VMEM((ROWS, HD), F32),
            pltpu.VMEM((32, HD), F32),
            pltpu.SemaphoreType.DMA((8,)),
        ],
        flops=2 * 72 * 32 * 256 * 128 * 2,
        nbytes=9000000,
    )(
        cache_lengths, slots, parts, all_ids, wq, wv, query_base.reshape(TOK, D), kvb, kv,
        arr0, arr1, arr2, arr3,
    )
    return out.reshape(STEPS, REQ, D)


def solution(mesh):
    return jax.shard_map(
        local,
        mesh=mesh,
        in_specs=(
            P(None, "rep", "tp"),
            P(None, "rep", "tp"),
            P(None, "rep", None, "tp"),
            P("rep", None, None, "tp"),
            P("rep"),
            P(None, "rep"),
            P(None, "rep"),
            P(),
            P(),
            P(None, None, None, "tp"),
            P(None, None, "tp"),
            P(None, None, "tp"),
            P("rep", None, None, "tp"),
            P("rep", None, "tp"),
            P("rep", None, "tp"),
        ),
        out_specs=P(None, "rep", "tp"),
        check_vma=False,
    )
```
